32 devices in a mesh: dp: 8 (over y, x, core), group: 4 (over z).
Axes of the slice: x: 2, y: 2, z: 4, core: 2. Of those that a mesh axis runs over, the one named last changes fastest.
Arguments:
- inputs: float32 [4096, 768], P(('dp', 'group')), may hold values from -6 to 6
- cotangent: float32 [4096, 768], P(('dp', 'group')), may hold values from -6 to 6
- lengths: int32 [32, 4], P(('dp', 'group')), may hold values from 1 to 64, 128 in all within a row
- attn_weights: float32 [4, 768, 768], P('group', 'dp'), may hold values from -1 to 1
- attn_momenta: float32 [4, 768, 768], P('group', 'dp'), may hold values from -1 to 1
- ffn_weights: float32 [2, 768, 3072], P(None, 'dp', 'group'), may hold values from -1 to 1
- ffn_momenta: float32 [2, 768, 3072], P(None, 'dp', 'group'), may hold values from -1 to 1
- vectors: float32 [12, 768], replicated, may hold values from -2 to 2
- vector_momenta: float32 [12, 768], replicated, may hold values from -1 to 1
Outputs:
- outputs: float32 [4096, 768], P(('dp', 'group'))
- input_grad: float32 [4096, 768], P(('dp', 'group'))
- attn_grads: float32 [4, 768, 768], P('group', 'dp')
- ffn_grads: float32 [2, 768, 3072], P(None, 'dp', 'group')
- vector_grads: float32 [12, 768], replicated
- new_attn_weights: float32 [4, 768, 768], P('group', 'dp')
- new_attn_momenta: float32 [4, 768, 768], P('group', 'dp')
- new_ffn_weights: float32 [2, 768, 3072], P(None, 'dp', 'group')
- new_ffn_momenta: float32 [2, 768, 3072], P(None, 'dp', 'group')
- new_vectors: float32 [12, 768], replicated
- new_vector_momenta: float32 [12, 768], replicated
The draws below stay inside these ranges and needn't reach their ends.
Inputs may be any that keep to these rules, and one draw needn't show every extreme that they name: Each device's 4 lengths sum to 128.
All inputs are finite; a program needn't handle non-finite values.
Results may differ from the reference program's by a relative error of at most 0.025.
The reference program's roundings to bfloat16 on the way count: a program that leaves them out, or rounds other values in their place, can miss the bound.
Values may be sent and summed in bfloat16 or wider, within the bound.
A program may use at most 128 MiB of HBM per device.

```python
import math
import jax
import jax.numpy as jnp
import numpy as np
from jax import lax

D = 768
HEADS = 12
FF = 3072
TOK_DEV = 128
SEQ_DEV = 4
MOST = 64
NS_ITERS = 3
TOKENS = 4096
N_DP = 8
N_GROUP = 4


def rising_scale(key, count):
    place = jnp.arange(count, dtype=jnp.float32) / float(max(count - 1, 1))
    ramp = jnp.exp(math.log(3.0) * (place - 0.5))
    jitter = jnp.exp(jax.random.uniform(key, (count,), jnp.float32, -0.6, 0.6))
    return ramp * jitter


def draw_attn_weights(key, part):
    scales = jnp.array([1.0, 1.0, 1.0, 4.0], jnp.float32) * D ** (-0.5)
    first = jax.random.normal(jax.random.fold_in(key, 11), (4, D, D), jnp.float32)
    values = first * scales[:, None, None]
    return jnp.clip(values, -1.0, 1.0)


def draw_attn_momenta(key, part):
    scales = jnp.array([0.5, 0.5, 1.0, 0.5], jnp.float32) / math.sqrt(TOKENS)
    rows = rising_scale(jax.random.fold_in(key, 23), D)
    values = jax.random.normal(jax.random.fold_in(key, 21), (4, D, D), jnp.float32)
    return jnp.clip(values * scales[:, None, None] * rows[None, :, None], -1.0, 1.0)


def draw_ffn_weights(key, part):
    scales = jnp.array([D ** (-0.5), 1.5 * FF ** (-0.5)], jnp.float32)
    values = jax.random.normal(jax.random.fold_in(key, 51), (2, D, FF), jnp.float32)
    return jnp.clip(values * scales[:, None, None], -1.0, 1.0)


def draw_ffn_momenta(key, part):
    scales = jnp.array([0.4, 0.8], jnp.float32) / math.sqrt(TOKENS)
    rows = rising_scale(jax.random.fold_in(key, 63), D)
    columns = rising_scale(jax.random.fold_in(key, 64), FF)
    values = jax.random.normal(jax.random.fold_in(key, 61), (2, D, FF), jnp.float32)
    values = values * scales[:, None, None] * rows[None, :, None] * columns[None, None, :]
    return jnp.clip(values, -1.0, 1.0)


def draw_vectors(key, part):
    count = 8 + FF // D
    row_index = jnp.arange(count, dtype=jnp.int32)
    is_gain = (row_index == 0) | (row_index == 5)
    offset = jnp.where(is_gain, 1.0, 0.0).astype(jnp.float32)
    spread = jnp.where(is_gain, 0.3, 0.5).astype(jnp.float32)
    base = jax.random.normal(jax.random.fold_in(key, 31), (count, D), jnp.float32)
    return jnp.clip(offset[:, None] + spread[:, None] * base, -2.0, 2.0)


def draw_vector_momenta(key, part):
    count = 8 + FF // D
    scale = 1.0 / math.sqrt(TOKENS)
    values = jax.random.normal(jax.random.fold_in(key, 41), (count, D), jnp.float32) * scale
    return jnp.clip(values, -1.0, 1.0)


def block_scale(rng, shape, split, low, largest):
    def one(dim, shards_of):
        steps = jax.random.uniform(jax.random.fold_in(jax.random.fold_in(rng, 6), dim), (shards_of,), jnp.float32, low / len(split), largest / len(split))
        return jnp.repeat(jnp.exp(steps), shape[dim] // shards_of).reshape((-1,) + (1,) * (len(shape) - dim - 1))

    loudness = one(*split[0])
    for cut in split[1:]:
        loudness = loudness * one(*cut)
    return loudness


def split_up(amount, total, limit, skew):
    portions = [(1 << 20) // math.isqrt(rank ** skew) + 1 for rank in range(2, amount + 1)]
    spare, counts = total - limit - (amount - 1), [1] * (amount - 1)
    while spare > 0:
        candidates = [i for i in range(amount - 1) if counts[i] < limit]
        whole, left = sum([portions[i] for i in candidates]), spare
        for i in candidates:
            extra = min(limit - counts[i], max(1, left * portions[i] // whole), spare)
            counts[i] = counts[i] + extra
            spare = spare - extra
    return np.array([limit] + counts)


def uneven(rng, count, total, limit, skew):
    if count == 2:
        one = jax.random.randint(rng, (), max(1, total - limit), min(limit, total - 1) + 1)
        return jnp.stack([one, total - one])
    tallies = jnp.asarray(split_up(count, total, limit, skew), jnp.int32)
    couples = (count - 1) // 2
    giver, receiver = tallies[1:1 + 2 * couples:2], tallies[2:2 + 2 * couples:2]
    margin = jnp.minimum(giver - 1, limit - receiver)
    passed = jax.random.randint(jax.random.fold_in(rng, 1), (couples,), 0, 1 << 20) % (margin + 1)
    tallies = tallies.at[1:1 + 2 * couples:2].set(giver - passed).at[2:2 + 2 * couples:2].set(receiver + passed)
    return tallies[jax.random.permutation(jax.random.fold_in(rng, 2), count)]


def gaussian(own_key, shape, scale, reach, shards=(), held_as=jnp.bfloat16):
    gain = block_scale(own_key, shape, shards, -0.22, 0.18) if shards else 1.0
    values = jax.random.normal(own_key, shape, jnp.float32) * scale * gain
    return jnp.minimum(jnp.maximum(values, -reach), reach).astype(held_as)


def setup_inputs(seed: int = 0) -> dict:
    key_list = jax.random.split(jax.random.key(seed), 10)
    inputs = gaussian(key_list[0], (TOKENS, D), 1.0, 6.0, ((0, 32),), jnp.float32)
    cotangent = gaussian(key_list[1], (TOKENS, D), 1.0, 6.0, ((0, 32),), jnp.float32)
    lengths = jax.vmap(lambda own: uneven(own, SEQ_DEV, TOK_DEV, MOST, 2))(jax.random.split(key_list[2], (N_DP * N_GROUP))).reshape((N_DP * N_GROUP, SEQ_DEV)).astype(jnp.int32)
    attn_weights = draw_attn_weights(jax.random.fold_in(key_list[9], 71), 0)
    attn_momenta = draw_attn_momenta(jax.random.fold_in(key_list[9], 71), 0)
    ffn_weights = draw_ffn_weights(jax.random.fold_in(key_list[9], 71), 0)
    ffn_momenta = draw_ffn_momenta(jax.random.fold_in(key_list[9], 71), 0)
    vectors = draw_vectors(jax.random.fold_in(key_list[9], 71), 0)
    vector_momenta = draw_vector_momenta(jax.random.fold_in(key_list[9], 71), 0)
    return {"inputs": inputs, "cotangent": cotangent, "lengths": lengths, "attn_weights": attn_weights, "attn_momenta": attn_momenta, "ffn_weights": ffn_weights, "ffn_momenta": ffn_momenta, "vectors": vectors, "vector_momenta": vector_momenta}


coef_first = 3.4445
coef_second = -4.775
coef_third = 2.0315
momentum_rate = 0.9
muon_rate = 0.8
vector_rate = 0.1

def norm_forward(rows):
    centre = lax.optimization_barrier(jnp.mean(rows, axis=1, keepdims=True))
    centred = rows - centre
    variance = lax.optimization_barrier(jnp.mean(centred * centred, axis=1, keepdims=True))
    inverse = lax.rsqrt(variance + 1e-05)
    return (centred * inverse, inverse)

def norm_backward(grad_normed, normed, inverse):
    return inverse * (grad_normed - lax.optimization_barrier(jnp.mean(grad_normed, axis=1, keepdims=True)) - normed * lax.optimization_barrier(jnp.mean(grad_normed * normed, axis=1, keepdims=True)))

def masked_scores(query_heads, key_heads, allowed):
    scores = jnp.einsum('qhd,khd->hqk', query_heads.astype(jnp.float32), key_heads.astype(jnp.float32))
    return jnp.where(allowed[None], scores, -jnp.inf)

def layer_block(block_rows, block_cotan, seq_lengths, attn_w, ffn_w, vectors):
    token_count = block_rows.shape[0]
    width = block_rows.shape[1]
    head_size = width // HEADS
    scale = 1.0 / math.sqrt(head_size)
    w_query, w_key, w_value, w_output = (attn_w[0], attn_w[1], attn_w[2], attn_w[3])
    w_expand, w_reduce = (ffn_w[0], ffn_w[1])
    expand_bias = vectors[8:].reshape(-1)
    positions = jnp.arange(token_count, dtype=jnp.int32)
    seq_ends = jnp.cumsum(seq_lengths.astype(jnp.int32)).astype(jnp.int32)
    segment = lax.optimization_barrier(jnp.sum((positions[:, None] >= seq_ends[None, :]).astype(jnp.int32), axis=1))
    allowed = (segment[:, None] == segment[None, :]) & (positions[None, :] <= positions[:, None])
    normed_first, inverse_first = norm_forward(block_rows)
    hidden_first = (normed_first * vectors[0] + vectors[1]).astype(jnp.bfloat16)
    query = ((jnp.dot(hidden_first, w_query, preferred_element_type=jnp.float32) + vectors[2]) * scale).astype(jnp.bfloat16)
    keyed = jnp.dot(hidden_first, w_key, preferred_element_type=jnp.float32).astype(jnp.bfloat16)
    valued = (jnp.dot(hidden_first, w_value, preferred_element_type=jnp.float32) + vectors[3]).astype(jnp.bfloat16)
    query_heads = query.reshape(token_count, HEADS, head_size)
    key_heads = keyed.reshape(token_count, HEADS, head_size)
    value_heads = valued.reshape(token_count, HEADS, head_size)
    scores = masked_scores(query_heads, key_heads, allowed)
    highest = lax.optimization_barrier(jnp.max(scores, axis=2, keepdims=True))
    log_total = highest + jnp.log(lax.optimization_barrier(jnp.sum(jnp.exp(scores - highest), axis=2, keepdims=True)))
    probs_first = jnp.exp(scores - log_total).astype(jnp.bfloat16)
    attended = jnp.einsum('hqk,khd->qhd', probs_first.astype(jnp.float32), value_heads.astype(jnp.float32))
    attended = attended.reshape(token_count, width).astype(jnp.bfloat16)
    middle = block_rows + jnp.dot(attended, w_output, preferred_element_type=jnp.float32) + vectors[4]
    normed_second, inverse_second = norm_forward(middle)
    hidden_second = (normed_second * vectors[5] + vectors[6]).astype(jnp.bfloat16)
    before = jnp.dot(hidden_second, w_expand, preferred_element_type=jnp.float32) + expand_bias
    active = jnp.maximum(before, 0.0).astype(jnp.bfloat16)
    outputs = middle + jnp.dot(active, w_reduce.T, preferred_element_type=jnp.float32) + vectors[7]
    cotan_b = block_cotan.astype(jnp.bfloat16)
    grad_reduce = jnp.dot(cotan_b.T, active, preferred_element_type=jnp.float32)
    grad_active = jnp.dot(cotan_b, w_reduce, preferred_element_type=jnp.float32)
    grad_before = jnp.where(before > 0.0, grad_active, 0.0)
    before_grad_b = grad_before.astype(jnp.bfloat16)
    grad_expand = jnp.dot(hidden_second.T, before_grad_b, preferred_element_type=jnp.float32)
    grad_second = jnp.dot(before_grad_b, w_expand.T, preferred_element_type=jnp.float32)
    grad_middle = block_cotan + norm_backward(grad_second * vectors[5], normed_second, inverse_second)
    middle_b = grad_middle.astype(jnp.bfloat16)
    grad_output_w = jnp.dot(attended.T, middle_b, preferred_element_type=jnp.float32)
    grad_attended = jnp.dot(middle_b, w_output.T, preferred_element_type=jnp.float32).astype(jnp.bfloat16)
    attended_heads = grad_attended.reshape(token_count, HEADS, head_size).astype(jnp.float32)
    probs = jnp.exp(masked_scores(query_heads, key_heads, allowed) - log_total)
    probs_b = probs.astype(jnp.bfloat16)
    grad_probs = jnp.einsum('qhd,khd->hqk', attended_heads, value_heads.astype(jnp.float32))
    grad_value = jnp.einsum('hqk,qhd->khd', probs_b.astype(jnp.float32), attended_heads)
    delta = lax.optimization_barrier(jnp.sum(probs * grad_probs, axis=2, keepdims=True))
    grad_scores = (probs * (grad_probs - delta)).astype(jnp.bfloat16).astype(jnp.float32)
    grad_query = jnp.einsum('hqk,khd->qhd', grad_scores, key_heads.astype(jnp.float32)) * scale
    grad_key = jnp.einsum('hqk,qhd->khd', grad_scores, query_heads.astype(jnp.float32))
    query_grad = grad_query.reshape(token_count, width)
    key_grad = grad_key.reshape(token_count, width)
    value_grad = grad_value.reshape(token_count, width)
    query_grad_b = query_grad.astype(jnp.bfloat16)
    key_grad_b = key_grad.astype(jnp.bfloat16)
    value_grad_b = value_grad.astype(jnp.bfloat16)
    grad_wq = jnp.dot(hidden_first.T, query_grad_b, preferred_element_type=jnp.float32)
    grad_wk = jnp.dot(hidden_first.T, key_grad_b, preferred_element_type=jnp.float32)
    grad_wv = jnp.dot(hidden_first.T, value_grad_b, preferred_element_type=jnp.float32)
    grad_first = jnp.dot(query_grad_b, w_query.T, preferred_element_type=jnp.float32)
    grad_first = grad_first + jnp.dot(key_grad_b, w_key.T, preferred_element_type=jnp.float32)
    grad_first = grad_first + jnp.dot(value_grad_b, w_value.T, preferred_element_type=jnp.float32)
    input_grad = grad_middle + norm_backward(grad_first * vectors[0], normed_first, inverse_first)
    attn_terms = jnp.stack([grad_wq, grad_wk, grad_wv, grad_output_w])
    ffn_terms = jnp.stack([grad_expand, grad_reduce])
    small_terms = jnp.stack([lax.optimization_barrier(jnp.sum(grad_first * normed_first, axis=0)), lax.optimization_barrier(jnp.sum(grad_first, axis=0)), lax.optimization_barrier(jnp.sum(query_grad, axis=0)), lax.optimization_barrier(jnp.sum(value_grad, axis=0)), lax.optimization_barrier(jnp.sum(grad_middle, axis=0)), lax.optimization_barrier(jnp.sum(grad_second * normed_second, axis=0)), lax.optimization_barrier(jnp.sum(grad_second, axis=0)), lax.optimization_barrier(jnp.sum(block_cotan, axis=0))])
    bias_terms = lax.optimization_barrier(jnp.sum(grad_before, axis=0)).reshape(-1, width)
    vector_terms = jnp.concatenate([small_terms, bias_terms], axis=0)
    return (outputs, input_grad, attn_terms, ffn_terms, vector_terms)

def orthogonalize(matrix):
    norm_value = jnp.sqrt(jnp.sum(matrix * matrix))
    iterate = matrix / (norm_value + 1e-07)
    for iteration in range(NS_ITERS):
        iterate_b = iterate.astype(jnp.bfloat16)
        gram = jnp.dot(iterate_b, iterate_b.T, preferred_element_type=jnp.float32)
        gram_b = gram.astype(jnp.bfloat16)
        mixed = coef_second * gram + coef_third * jnp.dot(gram_b, gram_b, preferred_element_type=jnp.float32)
        iterate = coef_first * iterate + jnp.dot(mixed.astype(jnp.bfloat16), iterate_b, preferred_element_type=jnp.float32)
    return iterate

def reference(inputs, cotangent, lengths, attn_weights, attn_momenta, ffn_weights, ffn_momenta, vectors, vector_momenta):
    width = inputs.shape[1]
    device_count = lengths.shape[0]
    attn_b = attn_weights.astype(jnp.bfloat16)
    ffn_b = ffn_weights.astype(jnp.bfloat16)

    def visit(carry, pieces):
        attn_sum, ffn_sum, vector_sum = carry
        block_rows, block_cotan, seq_lengths = pieces
        outputs, input_grad, attn_terms, ffn_terms, vector_terms = layer_block(block_rows, block_cotan, seq_lengths, attn_b, ffn_b, vectors)
        return ((attn_sum + attn_terms, ffn_sum + ffn_terms, vector_sum + vector_terms), (outputs, input_grad))
    start_carry = (jnp.zeros(attn_weights.shape, jnp.float32), jnp.zeros(ffn_weights.shape, jnp.float32), jnp.zeros(vectors.shape, jnp.float32))
    pieces = (inputs.reshape(device_count, TOK_DEV, width), cotangent.reshape(device_count, TOK_DEV, width), lengths)
    (attn_sum, ffn_sum, vector_sum), (outputs, input_grad) = lax.scan(visit, start_carry, pieces)
    outputs = outputs.reshape(device_count * TOK_DEV, width)
    input_grad = input_grad.reshape(device_count * TOK_DEV, width)
    attn_grads = attn_sum / float(TOKENS)
    ffn_grads = ffn_sum / float(TOKENS)
    vector_grads = vector_sum / float(TOKENS)
    new_attn_momenta = momentum_rate * attn_momenta + attn_grads
    new_ffn_momenta = momentum_rate * ffn_momenta + ffn_grads
    new_attn_weights = attn_weights - muon_rate * lax.map(orthogonalize, new_attn_momenta)
    new_ffn_weights = ffn_weights - muon_rate * lax.map(orthogonalize, new_ffn_momenta)
    new_vector_momenta = momentum_rate * vector_momenta + vector_grads
    spread = lax.rsqrt(lax.optimization_barrier(jnp.mean(new_vector_momenta * new_vector_momenta, axis=1, keepdims=True)) + 1e-06)
    new_vectors = vectors - vector_rate * new_vector_momenta * spread
    return (outputs, input_grad, attn_grads, ffn_grads, vector_grads, new_attn_weights, new_attn_momenta, new_ffn_weights, new_ffn_momenta, new_vectors, new_vector_momenta)
```

```python
import math

import jax
import jax.numpy as jnp
from jax import lax
from jax.experimental import pallas as pl
from jax.experimental.pallas import tpu as pltpu
from jax.sharding import PartitionSpec as P

HEADS = 12
NS_ITERS = 3


coef_first = 3.4445
coef_second = -4.775
coef_third = 2.0315
momentum_rate = 0.9
muon_rate = 0.8
vector_rate = 0.1


def norm_forward(rows):
    centre = jnp.mean(rows, axis=1, keepdims=True)
    centred = rows - centre
    variance = jnp.mean(centred * centred, axis=1, keepdims=True)
    inverse = lax.rsqrt(variance + 1e-05)
    return (centred * inverse, inverse)


def norm_backward(grad_normed, normed, inverse):
    return inverse * (
        grad_normed
        - jnp.mean(grad_normed, axis=1, keepdims=True)
        - normed * jnp.mean(grad_normed * normed, axis=1, keepdims=True)
    )


def masked_scores(query_heads, key_heads, allowed):
    scores = jnp.einsum("qhd,khd->hqk", query_heads, key_heads, preferred_element_type=jnp.float32)
    return jnp.where(allowed[None], scores, -jnp.inf)


MESH = pl.DeviceIdType.MESH


def flip(index, bits):
    result = index
    for bit in (1, 2, 4):
        if bits & bit:
            result = result + bit - 2 * bit * ((index // bit) % 2)
    return result


def out_struct(kind, x, n_group):
    if kind == "zag":
        shape = (n_group,) + x.shape
    elif kind == "za2a":
        shape = x.shape
    elif kind == "dpag":
        shape = (8,) + x.shape
    elif kind == "dprow":
        shape = (x.shape[0], 8 * x.shape[1], x.shape[2])
    elif kind == "dpscatter":
        shape = (8, x.shape[0], x.shape[1] // 8, x.shape[2])
    return jax.ShapeDtypeStruct(shape, x.dtype)


def exchange_kernel(kinds, n_group, *refs):
    count = len(kinds)
    ins, outs = refs[:count], refs[count : 2 * count]
    send_sem, recv_sem = refs[2 * count :]
    z = lax.axis_index("group")
    d = lax.axis_index("dp")
    z_used = any(kind[0] == "z" for kind in kinds)
    dp_used = any(kind[0] == "d" for kind in kinds)

    def z_peer(k):
        return lax.rem(z + k, n_group)

    barrier = pltpu.get_barrier_semaphore()
    greeted = 0
    if z_used:
        for k in range(1, n_group):
            pl.semaphore_signal(
                barrier, inc=1, device_id={"group": z_peer(k)}, device_id_type=MESH
            )
            greeted += 1
    if dp_used:
        for k in range(1, 8):
            pl.semaphore_signal(barrier, inc=1, device_id={"dp": flip(d, k)}, device_id_type=MESH)
            greeted += 1
    pl.semaphore_wait(barrier, greeted)

    slot = [0]

    def send(src, dst, device):
        copy = pltpu.make_async_remote_copy(
            src_ref=src,
            dst_ref=dst,
            send_sem=send_sem.at[slot[0]],
            recv_sem=recv_sem.at[slot[0]],
            device_id=device,
            device_id_type=MESH,
        )
        slot[0] += 1
        copy.start()
        return copy

    pending = []
    staged = []
    for kind, x, o in zip(kinds, ins, outs):
        if kind == "dprow":
            rows = x.shape[1]

            def place(index, part=None, o=o, rows=rows):
                start = pl.multiple_of(index * rows, rows)
                if part is None:
                    return o.at[:, pl.ds(start, rows), :]
                half = rows // 2
                start = pl.multiple_of(index * rows + part * half, half)
                return o.at[:, pl.ds(start, half), :]

            along_x = send(x, place(d), {"dp": flip(d, 2)})
            along_y = send(x, place(d), {"dp": flip(d, 4)})
            sibling = send(x, place(d), {"dp": flip(d, 1)})
            staged.append((place, along_x, along_y, sibling))
        elif kind == "dpag":
            for k in range(1, 8):
                pending.append(send(x, o.at[d], {"dp": flip(d, k)}))
        elif kind == "dpscatter":
            rows = x.shape[1] // 8
            for k in (6, 7, 2, 3, 4, 5, 1):
                peer = flip(d, k)
                start = pl.multiple_of(peer * rows, rows)
                pending.append(send(x.at[:, pl.ds(start, rows), :], o.at[d], {"dp": peer}))
        elif kind == "zag":
            for k in range(1, n_group):
                pending.append(send(x, o.at[z], {"group": z_peer(k)}))
        elif kind == "za2a":
            for k in range(1, n_group):
                pending.append(send(x.at[z_peer(k)], o.at[z], {"group": z_peer(k)}))
    for kind, x, o in zip(kinds, ins, outs):
        if kind == "dprow":
            rows = x.shape[1]
            o[:, pl.ds(pl.multiple_of(d * rows, rows), rows), :] = x[...]
        elif kind == "dpag":
            o[d] = x[...]
        elif kind == "dpscatter":
            rows = x.shape[1] // 8
            o[d] = x[:, pl.ds(pl.multiple_of(d * rows, rows), rows), :]
        elif kind == "zag":
            o[z] = x[...]
        elif kind == "za2a":
            o[z] = x[z]
    second = []
    for place, along_x, along_y, sibling in staged:
        along_x.wait_recv()
        from_x = flip(d, 2)
        to_y = send(place(from_x, 0), place(from_x, 0), {"dp": flip(d, 4)})
        share_x = send(place(from_x), place(from_x), {"dp": flip(d, 1)})
        along_y.wait_recv()
        from_y = flip(d, 4)
        to_x = send(place(from_y, 1), place(from_y, 1), {"dp": flip(d, 2)})
        share_y = send(place(from_y), place(from_y), {"dp": flip(d, 1)})
        second.append((place, along_x, along_y, sibling, to_y, share_x, to_x, share_y))
    for place, along_x, along_y, sibling, to_y, share_x, to_x, share_y in second:
        to_y.wait_recv()
        to_x.wait_recv()
        far = flip(d, 6)
        share_far = send(place(far), place(far), {"dp": flip(d, 1)})
        for copy in (sibling, share_x, share_y):
            copy.wait()
        for copy in (along_x, along_y, to_y, to_x):
            copy.wait_send()
        share_far.wait()
    for copy in pending:
        copy.wait()


def exchange(collective_id, *pairs):
    n_group = lax.axis_size("group")
    kinds = tuple(kind for kind, _ in pairs)
    arrays = [x for _, x in pairs]
    if lax.axis_size("dp") != 8:
        results = []
        for kind, x in pairs:
            if kind == "zag":
                results.append(lax.all_gather(x, "group", axis=0))
            elif kind == "za2a":
                results.append(lax.all_to_all(x, "group", 0, 0))
            elif kind == "dpag":
                results.append(lax.all_gather(x, "dp", axis=0))
            elif kind == "dprow":
                results.append(lax.all_gather(x, "dp", axis=1, tiled=True))
            elif kind == "dpscatter":
                n_dp = lax.axis_size("dp")
                cut = x.reshape(x.shape[0], n_dp, x.shape[1] // n_dp, x.shape[2])
                results.append(lax.all_to_all(cut.swapaxes(0, 1), "dp", 0, 0))
        return results
    copies = 0
    for kind in kinds:
        copies += {"zag": n_group - 1, "za2a": n_group - 1, "dprow": 8}.get(kind, 7)
    return pl.pallas_call(
        lambda *refs: exchange_kernel(kinds, n_group, *refs),
        out_shape=[out_struct(kind, x, n_group) for kind, x in pairs],
        in_specs=[pl.BlockSpec(memory_space=pltpu.VMEM)] * len(kinds),
        out_specs=[pl.BlockSpec(memory_space=pltpu.VMEM)] * len(kinds),
        scratch_shapes=[
            pltpu.SemaphoreType.DMA((copies,)),
            pltpu.SemaphoreType.DMA((copies,)),
        ],
        compiler_params=pltpu.CompilerParams(collective_id=collective_id, has_side_effects=True),
        name=f"exchange_{collective_id}",
    )(*arrays)


def mm(left, right, dims):
    return lax.dot_general(left, right, (dims, ((), ())), preferred_element_type=jnp.float32)


NN = ((1,), (0,))
NT = ((1,), (1,))
TN = ((0,), (0,))


def newton_schulz_rows(gram, own_rows, whole_b, row_start):
    rows = own_rows.shape[0]
    lead = 1.0
    spread = None
    for iteration in range(NS_ITERS):
        gram_b = gram.astype(jnp.bfloat16)
        mixed = coef_second * gram + coef_third * mm(gram_b, gram_b, NN)
        mixed_b = mixed.astype(jnp.bfloat16)
        if iteration < NS_ITERS - 1:
            half = coef_first * gram + mm(mixed_b, gram_b, NN)
            gram = coef_first * half + mm(half.astype(jnp.bfloat16), mixed_b, NN)
        if spread is None:
            spread = lax.dynamic_slice_in_dim(mixed, row_start, rows, 0)
        else:
            mine = lax.dynamic_slice_in_dim(mixed, row_start, rows, 0)
            spread = (
                coef_first * spread
                + lead * mine
                + mm(spread.astype(jnp.bfloat16), mixed_b, NN)
            )
        lead = lead * coef_first
    return lead * own_rows + mm(spread.astype(jnp.bfloat16), whole_b, NN)


def on_device(
    inputs,
    cotangent,
    lengths,
    attn_weights,
    attn_momenta,
    ffn_weights,
    ffn_momenta,
    vectors,
    vector_momenta,
):
    group_count = lax.axis_size("group")
    dp_count = lax.axis_size("dp")
    own_index = lax.axis_index("group")
    dp_index = lax.axis_index("dp")
    token_count, width = inputs.shape
    own_count = attn_weights.shape[1]
    quarter = ffn_weights.shape[2]
    head_size = width // HEADS
    scale = 1.0 / math.sqrt(head_size)
    bf16 = jnp.bfloat16

    own_attn = attn_weights.astype(bf16)
    own_ffn = ffn_weights.astype(bf16)
    cotan_b = cotangent.astype(bf16)
    (attn_rows,) = exchange(0, ("zag", own_attn[0]))
    weights, all_cotan = exchange(
        1, ("dprow", jnp.concatenate([attn_rows, own_ffn], axis=0)), ("zag", cotan_b)
    )
    w_query, w_key, w_value, w_output, w_expand, w_reduce = [weights[i] for i in range(6)]
    all_cotan = all_cotan.reshape(-1, width)

    positions = jnp.arange(token_count, dtype=jnp.int32)
    seq_ends = jnp.cumsum(lengths[0])
    segment = jnp.sum((positions[:, None] >= seq_ends[None, :]).astype(jnp.int32), axis=1)
    allowed = (segment[:, None] == segment[None, :]) & (positions[None, :] <= positions[:, None])
    normed_first, inverse_first = norm_forward(inputs)
    hidden_first = (normed_first * vectors[0] + vectors[1]).astype(bf16)
    query = ((mm(hidden_first, w_query, NN) + vectors[2]) * scale).astype(bf16)
    keyed = mm(hidden_first, w_key, NN).astype(bf16)
    valued = (mm(hidden_first, w_value, NN) + vectors[3]).astype(bf16)
    query_heads = query.reshape(token_count, HEADS, head_size)
    key_heads = keyed.reshape(token_count, HEADS, head_size)
    value_heads = valued.reshape(token_count, HEADS, head_size)
    scores = masked_scores(query_heads, key_heads, allowed)
    highest = jnp.max(scores, axis=2, keepdims=True)
    log_total = highest + jnp.log(jnp.sum(jnp.exp(scores - highest), axis=2, keepdims=True))
    probs = jnp.exp(scores - log_total)
    probs_b = probs.astype(bf16)
    attended = jnp.einsum("hqk,khd->qhd", probs_b, value_heads, preferred_element_type=jnp.float32)
    attended = attended.reshape(token_count, width).astype(bf16)
    middle = inputs + mm(attended, w_output, NN) + vectors[4]
    normed_second, inverse_second = norm_forward(middle)
    hidden_second = (normed_second * vectors[5] + vectors[6]).astype(bf16)

    (all_second,) = exchange(2, ("zag", hidden_second))
    all_second = all_second.reshape(-1, width)
    own_bias = lax.dynamic_slice_in_dim(vectors[8:].reshape(-1), own_index * quarter, quarter, 0)
    before = mm(all_second, w_expand, NN) + own_bias
    active = jnp.maximum(before, 0.0).astype(bf16)
    out_part = mm(active, w_reduce, NT).astype(bf16)
    grad_before = jnp.where(before > 0.0, mm(all_cotan, w_reduce, NN), 0.0)
    before_grad_b = grad_before.astype(bf16)
    second_part = mm(before_grad_b, w_expand, NT).astype(bf16)

    (second_parts,) = exchange(
        3, ("za2a", second_part.reshape(group_count, token_count, width))
    )
    grad_second = jnp.sum(second_parts.astype(jnp.float32), axis=0)
    grad_middle = cotangent + norm_backward(
        grad_second * vectors[5], normed_second, inverse_second
    )
    middle_b = grad_middle.astype(bf16)
    grad_attended = mm(middle_b, w_output, NT).astype(bf16)
    attended_heads = grad_attended.reshape(token_count, HEADS, head_size)
    grad_probs = jnp.einsum(
        "qhd,khd->hqk", attended_heads, value_heads, preferred_element_type=jnp.float32
    )
    grad_value = jnp.einsum(
        "hqk,qhd->khd", probs_b, attended_heads, preferred_element_type=jnp.float32
    )
    delta = jnp.sum(probs * grad_probs, axis=2, keepdims=True)
    grad_scores = (probs * (grad_probs - delta)).astype(bf16)
    grad_query = (
        jnp.einsum("hqk,khd->qhd", grad_scores, key_heads, preferred_element_type=jnp.float32)
        * scale
    )
    grad_key = jnp.einsum(
        "hqk,qhd->khd", grad_scores, query_heads, preferred_element_type=jnp.float32
    )
    query_grad = grad_query.reshape(token_count, width)
    key_grad = grad_key.reshape(token_count, width)
    value_grad = grad_value.reshape(token_count, width)
    query_grad_b = query_grad.astype(bf16)
    key_grad_b = key_grad.astype(bf16)
    value_grad_b = value_grad.astype(bf16)

    left, right = exchange(
        4,
        ("za2a", jnp.stack([hidden_first, hidden_first, hidden_first, attended])),
        ("za2a", jnp.stack([query_grad_b, key_grad_b, value_grad_b, middle_b])),
    )
    grad_first = (
        mm(query_grad_b, w_query, NT) + mm(key_grad_b, w_key, NT) + mm(value_grad_b, w_value, NT)
    )
    input_grad = grad_middle + norm_backward(grad_first * vectors[0], normed_first, inverse_first)
    small_terms = jnp.stack(
        [
            jnp.sum(grad_first * normed_first, axis=0),
            jnp.sum(grad_first, axis=0),
            jnp.sum(query_grad, axis=0),
            jnp.sum(value_grad, axis=0),
            jnp.sum(grad_middle, axis=0),
            jnp.sum(grad_second * normed_second, axis=0),
            jnp.sum(grad_second, axis=0),
            jnp.sum(cotangent, axis=0),
        ]
    )
    owner_mask = jnp.arange(group_count, dtype=jnp.int32) == own_index
    bias_terms = jnp.where(owner_mask[:, None], jnp.sum(grad_before, axis=0)[None], 0.0)
    vector_terms = jnp.concatenate([small_terms, bias_terms.reshape(-1, width)], axis=0)
    grad_terms = jnp.stack(
        [
            mm(left.reshape(-1, width), right.reshape(-1, width), TN).astype(bf16),
            mm(all_second, before_grad_b, TN).astype(bf16),
            mm(all_cotan, active, TN).astype(bf16),
        ]
    )
    vector_all, grad_all, out_parts = exchange(
        5,
        ("dpag", vector_terms),
        ("dpscatter", grad_terms),
        ("za2a", out_part.reshape(group_count, token_count, width)),
    )
    outputs = middle + jnp.sum(out_parts.astype(jnp.float32), axis=0) + vectors[7]
    total_tokens = float(token_count * dp_count * group_count)
    grad_total = jnp.sum(grad_all.astype(jnp.float32), axis=0) / total_tokens
    attn_grads = grad_total[:1]
    ffn_grads = grad_total[1:]
    attn_next = momentum_rate * attn_momenta + attn_grads
    ffn_next = momentum_rate * ffn_momenta + ffn_grads
    own_next = jnp.concatenate([attn_next, ffn_next], axis=0)
    squares = jnp.sum(own_next * own_next, axis=(1, 2))
    squares = jnp.broadcast_to(jnp.pad(squares, (0, 5))[:, None], (8, 128))

    next_full, square_all, vector_groups = exchange(
        6, ("dprow", own_next.astype(bf16)), ("dpag", squares), ("zag", jnp.sum(vector_all, axis=0))
    )
    square_plane = jnp.sum(square_all, axis=0)
    own_b = own_next.astype(bf16)
    gram_part = jnp.concatenate([mm(own_b[1], next_full[1], NT), mm(own_b[2], next_full[2], NT)])
    piece = 2 * own_count // group_count
    gram_pieces, square_groups = exchange(
        7, ("za2a", gram_part.reshape(group_count, piece, width)), ("zag", square_plane)
    )
    ffn_square = jnp.sum(square_groups, axis=0)[1:3, 0]
    attn_scale = 1.0 / (jnp.sqrt(square_plane[0, 0]) + 1e-07)
    ffn_scale = 1.0 / (jnp.sqrt(ffn_square) + 1e-07)
    piece_scale = jnp.where(own_index < group_count // 2, ffn_scale[0], ffn_scale[1])
    gram_piece = (jnp.sum(gram_pieces, axis=0) * (piece_scale * piece_scale)).astype(bf16)
    (gram_rows,) = exchange(8, ("zag", gram_piece))
    (gram_full,) = exchange(9, ("dprow", gram_rows.reshape(2, own_count, width)))

    row_start = dp_index * own_count
    attn_unit = next_full[0].astype(jnp.float32) * attn_scale
    attn_unit_b = attn_unit.astype(bf16)
    attn_gram = mm(attn_unit_b, attn_unit_b, NT)
    steps = [newton_schulz_rows(attn_gram, own_next[0] * attn_scale, attn_unit_b, row_start)]
    for i in range(2):
        unit_b = (next_full[1 + i].astype(jnp.float32) * ffn_scale[i]).astype(bf16)
        steps.append(
            newton_schulz_rows(
                gram_full[i].astype(jnp.float32), own_next[1 + i] * ffn_scale[i], unit_b, row_start
            )
        )
    new_attn_weights = attn_weights - muon_rate * steps[0][None]
    new_ffn_weights = ffn_weights - muon_rate * jnp.stack(steps[1:])
    vector_grads = jnp.sum(vector_groups, axis=0) / total_tokens
    new_vector_momenta = momentum_rate * vector_momenta + vector_grads
    mean_square = jnp.mean(new_vector_momenta * new_vector_momenta, axis=1, keepdims=True)
    new_vectors = vectors - vector_rate * new_vector_momenta * lax.rsqrt(mean_square + 1e-06)
    return (
        outputs,
        input_grad,
        attn_grads,
        ffn_grads,
        vector_grads,
        new_attn_weights,
        attn_next,
        new_ffn_weights,
        ffn_next,
        new_vectors,
        new_vector_momenta,
    )


def solution(mesh):
    in_specs = (
        P(("dp", "group"), None),
        P(("dp", "group"), None),
        P(("dp", "group"), None),
        P("group", "dp", None),
        P("group", "dp", None),
        P(None, "dp", "group"),
        P(None, "dp", "group"),
        P(),
        P(),
    )
    out_specs = (
        P(("dp", "group"), None),
        P(("dp", "group"), None),
        P("group", "dp", None),
        P(None, "dp", "group"),
        P(),
        P("group", "dp", None),
        P("group", "dp", None),
        P(None, "dp", "group"),
        P(None, "dp", "group"),
        P(),
        P(),
    )
    return jax.shard_map(
        on_device, mesh=mesh, in_specs=in_specs, out_specs=out_specs, check_vma=False
    )
```

```python
import math

import jax
import jax.numpy as jnp
from jax import lax
from jax.experimental import pallas as pl
from jax.experimental.pallas import tpu as pltpu
from jax.sharding import PartitionSpec as P

HEADS = 12
NS_ITERS = 3


coef_first = 3.4445
coef_second = -4.775
coef_third = 2.0315
momentum_rate = 0.9
muon_rate = 0.8
vector_rate = 0.1


def norm_forward(rows):
    centre = jnp.mean(rows, axis=1, keepdims=True)
    centred = rows - centre
    variance = jnp.mean(centred * centred, axis=1, keepdims=True)
    inverse = lax.rsqrt(variance + 1e-05)
    return (centred * inverse, inverse)


def norm_backward(grad_normed, normed, inverse):
    return inverse * (
        grad_normed
        - jnp.mean(grad_normed, axis=1, keepdims=True)
        - normed * jnp.mean(grad_normed * normed, axis=1, keepdims=True)
    )


def masked_scores(query_heads, key_heads, allowed):
    scores = jnp.einsum("qhd,khd->hqk", query_heads, key_heads, preferred_element_type=jnp.float32)
    return jnp.where(allowed[None], scores, -jnp.inf)


MESH = pl.DeviceIdType.MESH


def flip(index, bits):
    result = index
    for bit in (1, 2, 4):
        if bits & bit:
            result = result + bit - 2 * bit * ((index // bit) % 2)
    return result


def out_struct(kind, x, n_group):
    dtype = x.dtype
    if kind == "zag":
        shape = (n_group,) + x.shape
    elif kind == "za2a":
        shape = x.shape
    elif kind == "dpag":
        shape = (8,) + x.shape
    elif kind == "dprow":
        shape = (x.shape[0], 8 * x.shape[1], x.shape[2])
    elif kind == "dpscatter":
        shape = (x.shape[0], x.shape[1] // 8, x.shape[2])
        dtype = jnp.float32
    else:
        count = kind[1]
        shape = (count, 8 * (n_group // count) * x.shape[0], x.shape[1])
    return jax.ShapeDtypeStruct(shape, dtype)


def scratch_of(kind, x, n_group):
    if kind[0] == "chain":
        return [pltpu.VMEM((n_group,) + x.shape, x.dtype)]
    if kind == "dpscatter":
        count, rows, width = x.shape
        rows = rows // 8
        return [
            pltpu.VMEM((count, 4, rows, width), x.dtype),
            pltpu.VMEM((count, 4, rows, width), x.dtype),
            pltpu.VMEM((count, 4, rows // 2, width), x.dtype),
            pltpu.VMEM((count, 2, rows // 2, width), x.dtype),
            pltpu.VMEM((count, 2, rows // 2, width), x.dtype),
        ]
    return []


def copies_of(kind, x, n_group):
    if kind[0] == "chain":
        return n_group - 1 + 8 * n_group
    if kind == "dprow":
        return 8 * x.shape[0]
    if kind == "dpscatter":
        return 10 * x.shape[0]
    return 7 if kind == "dpag" else n_group - 1


def exchange_kernel(kinds, n_group, scratch_counts, *refs):
    count = len(kinds)
    ins, outs = refs[:count], refs[count : 2 * count]
    send_sem, recv_sem = refs[-2:]
    spare = list(refs[2 * count : -2])
    scratch = []
    for number in scratch_counts:
        scratch.append(spare[:number])
        spare = spare[number:]
    z = lax.axis_index("group")
    d = lax.axis_index("dp")
    z_used = any(kind[0] in ("z", "chain") for kind in kinds)
    dp_used = any(kind[0] in ("d", "chain") for kind in kinds)

    def z_peer(k):
        return lax.rem(z + k, n_group)

    barrier = pltpu.get_barrier_semaphore()
    greeted = 0
    if z_used:
        for k in range(1, n_group):
            pl.semaphore_signal(
                barrier, inc=1, device_id={"group": z_peer(k)}, device_id_type=MESH
            )
            greeted += 1
    if dp_used:
        for k in range(1, 8):
            pl.semaphore_signal(barrier, inc=1, device_id={"dp": flip(d, k)}, device_id_type=MESH)
            greeted += 1
    pl.semaphore_wait(barrier, greeted)

    slot = [0]

    def send(src, dst, device):
        copy = pltpu.make_async_remote_copy(
            src_ref=src,
            dst_ref=dst,
            send_sem=send_sem.at[slot[0]],
            recv_sem=recv_sem.at[slot[0]],
            device_id=device,
            device_id_type=MESH,
        )
        slot[0] += 1
        copy.start()
        return copy

    pending = []
    staged = []

    def spread(src, o, matrix, block, offset, rows):
        first = rows // 32 * 16

        def place(index, part=None):
            start = index * block + offset
            size = rows
            if part is not None:
                start = start + part * first
                size = (first, rows - first)[part]
            return o.at[matrix, pl.ds(pl.multiple_of(start, 16), size), :]

        along_x = send(src, place(d), {"dp": flip(d, 2)})
        along_y = send(src, place(d), {"dp": flip(d, 4)})
        sibling = send(src, place(d), {"dp": flip(d, 1)})
        staged.append((place, along_x, along_y, sibling))

    chained = []
    for kind, x, o, spare in zip(kinds, ins, outs, scratch):
        if kind[0] == "chain":
            copies = [
                send(x, spare[0].at[z], {"group": z_peer(k)}) for k in range(1, n_group)
            ]
            per = n_group // kind[1]
            chained.append((copies, x, o, spare[0], per))
            rows = x.shape[0]
            spread(x, o, z // per, per * rows, lax.rem(z, per) * rows, rows)
    scatters = []
    for kind, x, o, spare in zip(kinds, ins, outs, scratch):
        if kind == "dprow":
            rows = x.shape[1]
            for i in range(x.shape[0]):
                spread(x.at[i], o, i, rows, 0, rows)
        elif kind == "dpscatter":
            rows = x.shape[1] // 8
            for i in range(x.shape[0]):
                copies = []
                for r in (3, 1, 2, 0):
                    start = pl.multiple_of(flip(d, 2 * r + 1) * rows, rows)
                    copies.append(
                        send(
                            x.at[i, pl.ds(start, rows), :],
                            spare[0].at[i, r],
                            {"dp": flip(d, 1)},
                        )
                    )
                scatters.append((i, x, o, rows, spare, copies))
        elif kind == "dpag":
            for k in range(1, 8):
                pending.append(send(x, o.at[d], {"dp": flip(d, k)}))
    if not chained:
        start_z(kinds, ins, outs, z, z_peer, n_group, send, pending)

    for kind, x, o in zip(kinds, ins, outs):
        if kind[0] == "chain":
            per = n_group // kind[1]
            rows = x.shape[0]
            start = pl.multiple_of(d * per * rows + lax.rem(z, per) * rows, 16)
            o[z // per, pl.ds(start, rows), :] = x[...]
        elif kind == "dprow":
            rows = x.shape[1]
            o[:, pl.ds(pl.multiple_of(d * rows, rows), rows), :] = x[...]
        elif kind == "dpag":
            o[d] = x[...]
        elif kind == "zag":
            o[z] = x[...]
        elif kind == "za2a":
            o[z] = x[z]

    for copies, x, o, held, per in chained:
        rows = x.shape[0]
        for k in range(1, n_group):
            copies[k - 1].wait_recv()
            origin = lax.rem(z + n_group - k, n_group)
            offset = lax.rem(origin, per) * rows
            spread(held.at[origin], o, origin // per, per * rows, offset, rows)
            start = pl.multiple_of(d * per * rows + offset, 16)
            o[origin // per, pl.ds(start, rows), :] = held[origin]
    if chained:
        start_z(kinds, ins, outs, z, z_peer, n_group, send, pending)

    second = []
    for place, along_x, along_y, sibling in staged:
        along_x.wait_recv()
        from_x = flip(d, 2)
        to_y = send(place(from_x, 0), place(from_x, 0), {"dp": flip(d, 4)})
        share_x = send(place(from_x), place(from_x), {"dp": flip(d, 1)})
        along_y.wait_recv()
        from_y = flip(d, 4)
        to_x = send(place(from_y, 1), place(from_y, 1), {"dp": flip(d, 2)})
        share_y = send(place(from_y), place(from_y), {"dp": flip(d, 1)})
        second.append((place, (along_x, along_y, to_y, to_x), (sibling, share_x, share_y)))
    third = []
    for place, links, shares in second:
        links[2].wait_recv()
        links[3].wait_recv()
        far = flip(d, 6)
        third.append(send(place(far), place(far), {"dp": flip(d, 1)}))

    wide = jnp.float32
    level = []
    for i, x, o, rows, spare, copies in scatters:
        near, total, recv_b, recv_c, part = spare
        half = rows // 2
        low, high = pl.ds(0, half), pl.ds(half, half)
        for r, copy in zip((3, 1, 2, 0), copies):
            copy.wait_recv()
            start = pl.multiple_of(flip(d, 2 * r) * rows, rows)
            own = x[i, pl.ds(start, rows), :].astype(wide)
            total[i, r] = (own + near[i, r].astype(wide)).astype(total.dtype)
        to_x = {"dp": flip(d, 2)}
        to_y = {"dp": flip(d, 4)}
        moved = [
            send(total.at[i, 3, low], recv_b.at[i, 1], to_x),
            send(total.at[i, 3, high], recv_b.at[i, 3], to_y),
            send(total.at[i, 1, low], recv_b.at[i, 0], to_x),
            send(total.at[i, 2, high], recv_b.at[i, 2], to_y),
        ]
        level.append(moved)
    last = []
    for (i, x, o, rows, spare, copies), moved in zip(scatters, level):
        near, total, recv_b, recv_c, part = spare
        half = rows // 2
        low, high = pl.ds(0, half), pl.ds(half, half)
        moved[0].wait_recv()
        part[i, 0] = (
            total[i, 2, low].astype(wide) + recv_b[i, 1].astype(wide)
        ).astype(part.dtype)
        moved[1].wait_recv()
        part[i, 1] = (
            total[i, 1, high].astype(wide) + recv_b[i, 3].astype(wide)
        ).astype(part.dtype)
        last.append(
            (
                send(part.at[i, 0], recv_c.at[i, 0], {"dp": flip(d, 4)}),
                send(part.at[i, 1], recv_c.at[i, 1], {"dp": flip(d, 2)}),
            )
        )
    for (i, x, o, rows, spare, copies), moved, ends in zip(scatters, level, last):
        near, total, recv_b, recv_c, part = spare
        half = rows // 2
        low, high = pl.ds(0, half), pl.ds(half, half)
        moved[2].wait_recv()
        moved[3].wait_recv()
        ends[0].wait_recv()
        o[i, low, :] = (
            total[i, 0, low].astype(wide) + recv_b[i, 0].astype(wide) + recv_c[i, 0].astype(wide)
        )
        ends[1].wait_recv()
        o[i, high, :] = (
            total[i, 0, high].astype(wide) + recv_b[i, 2].astype(wide) + recv_c[i, 1].astype(wide)
        )
        for copy in (*copies, *moved, *ends):
            copy.wait_send()

    for copies, *_ in chained:
        for copy in copies:
            copy.wait_send()
    for place, links, shares in second:
        for copy in shares:
            copy.wait()
        for copy in links:
            copy.wait_send()
    for copy in third:
        copy.wait()
    for copy in pending:
        copy.wait()


def start_z(kinds, ins, outs, z, z_peer, n_group, send, pending):
    for kind, x, o in zip(kinds, ins, outs):
        for k in range(1, n_group):
            if kind == "zag":
                pending.append(send(x, o.at[z], {"group": z_peer(k)}))
            elif kind == "za2a":
                pending.append(send(x.at[z_peer(k)], o.at[z], {"group": z_peer(k)}))


def exchange(collective_id, *pairs):
    n_group = lax.axis_size("group")
    kinds = tuple(kind for kind, _ in pairs)
    arrays = [x for _, x in pairs]
    if lax.axis_size("dp") != 8:
        results = []
        for kind, x in pairs:
            if kind == "zag":
                results.append(lax.all_gather(x, "group", axis=0))
            elif kind == "za2a":
                results.append(lax.all_to_all(x, "group", 0, 0))
            elif kind == "dpag":
                results.append(lax.all_gather(x, "dp", axis=0))
            elif kind == "dprow":
                results.append(lax.all_gather(x, "dp", axis=1, tiled=True))
            elif kind == "dpscatter":
                wide = x.astype(jnp.float32)
                results.append(lax.psum_scatter(wide, "dp", scatter_dimension=1, tiled=True))
            else:
                held = lax.all_gather(x, "group", axis=0).reshape(kind[1], -1, x.shape[1])
                results.append(lax.all_gather(held, "dp", axis=1, tiled=True))
        return results
    copies = sum(copies_of(kind, x, n_group) for kind, x in pairs)
    scratch = [scratch_of(kind, x, n_group) for kind, x in pairs]
    scratch_counts = tuple(len(shapes) for shapes in scratch)
    return pl.pallas_call(
        lambda *refs: exchange_kernel(kinds, n_group, scratch_counts, *refs),
        out_shape=[out_struct(kind, x, n_group) for kind, x in pairs],
        in_specs=[pl.BlockSpec(memory_space=pltpu.VMEM)] * len(kinds),
        out_specs=[pl.BlockSpec(memory_space=pltpu.VMEM)] * len(kinds),
        scratch_shapes=[
            *[shape for shapes in scratch for shape in shapes],
            pltpu.SemaphoreType.DMA((copies,)),
            pltpu.SemaphoreType.DMA((copies,)),
        ],
        compiler_params=pltpu.CompilerParams(collective_id=collective_id, has_side_effects=True),
        name=f"exchange_{collective_id}",
    )(*arrays)


def mm(left, right, dims):
    return lax.dot_general(left, right, (dims, ((), ())), preferred_element_type=jnp.float32)


NN = ((1,), (0,))
NT = ((1,), (1,))
TN = ((0,), (0,))


def newton_schulz_rows(gram, own_rows, whole_b, row_start):
    rows = own_rows.shape[0]
    lead = 1.0
    spread = None
    for iteration in range(NS_ITERS - 1):
        gram_b = gram.astype(jnp.bfloat16)
        mixed = coef_second * gram + coef_third * mm(gram_b, gram_b, NN)
        mixed_b = mixed.astype(jnp.bfloat16)
        half = coef_first * gram + mm(mixed_b, gram_b, NN)
        gram = coef_first * half + mm(half.astype(jnp.bfloat16), mixed_b, NN)
        mine = lax.dynamic_slice_in_dim(mixed, row_start, rows, 0)
        if spread is None:
            spread = mine
        else:
            product = mm(spread.astype(jnp.bfloat16), mixed_b, NN)
            spread = coef_first * spread + lead * mine + product
        lead = lead * coef_first
    gram_b = gram.astype(jnp.bfloat16)
    once = lead * lax.dynamic_slice_in_dim(gram, row_start, rows, 0) + mm(
        spread.astype(jnp.bfloat16), gram_b, NN
    )
    twice = mm(once.astype(jnp.bfloat16), gram_b, NN)
    spread = coef_first * spread + coef_second * once + coef_third * twice
    lead = lead * coef_first
    return lead * own_rows + mm(spread.astype(jnp.bfloat16), whole_b, NN)


def on_device(
    inputs,
    cotangent,
    lengths,
    attn_weights,
    attn_momenta,
    ffn_weights,
    ffn_momenta,
    vectors,
    vector_momenta,
):
    group_count = lax.axis_size("group")
    dp_count = lax.axis_size("dp")
    own_index = lax.axis_index("group")
    dp_index = lax.axis_index("dp")
    token_count, width = inputs.shape
    own_count = attn_weights.shape[1]
    quarter = ffn_weights.shape[2]
    head_size = width // HEADS
    scale = 1.0 / math.sqrt(head_size)
    bf16 = jnp.bfloat16

    own_attn = attn_weights.astype(bf16)
    own_ffn = ffn_weights.astype(bf16)
    cotan_b = cotangent.astype(bf16)
    attn_full, ffn_full, all_cotan = exchange(
        0, (("chain", 4), own_attn[0]), ("dprow", own_ffn), ("zag", cotan_b)
    )
    w_query, w_key, w_value, w_output = [attn_full[i] for i in range(4)]
    w_expand, w_reduce = [ffn_full[i] for i in range(2)]
    all_cotan = all_cotan.reshape(-1, width)

    positions = jnp.arange(token_count, dtype=jnp.int32)
    seq_ends = jnp.cumsum(lengths[0])
    segment = jnp.sum((positions[:, None] >= seq_ends[None, :]).astype(jnp.int32), axis=1)
    allowed = (segment[:, None] == segment[None, :]) & (positions[None, :] <= positions[:, None])
    normed_first, inverse_first = norm_forward(inputs)
    hidden_first = (normed_first * vectors[0] + vectors[1]).astype(bf16)
    query = ((mm(hidden_first, w_query, NN) + vectors[2]) * scale).astype(bf16)
    keyed = mm(hidden_first, w_key, NN).astype(bf16)
    valued = (mm(hidden_first, w_value, NN) + vectors[3]).astype(bf16)
    query_heads = query.reshape(token_count, HEADS, head_size)
    key_heads = keyed.reshape(token_count, HEADS, head_size)
    value_heads = valued.reshape(token_count, HEADS, head_size)
    scores = masked_scores(query_heads, key_heads, allowed)
    highest = jnp.max(scores, axis=2, keepdims=True)
    log_total = highest + jnp.log(jnp.sum(jnp.exp(scores - highest), axis=2, keepdims=True))
    probs = jnp.exp(scores - log_total)
    probs_b = probs.astype(bf16)
    attended = jnp.einsum("hqk,khd->qhd", probs_b, value_heads, preferred_element_type=jnp.float32)
    attended = attended.reshape(token_count, width).astype(bf16)
    middle = inputs + mm(attended, w_output, NN) + vectors[4]
    normed_second, inverse_second = norm_forward(middle)
    hidden_second = (normed_second * vectors[5] + vectors[6]).astype(bf16)

    (all_second,) = exchange(2, ("zag", hidden_second))
    all_second = all_second.reshape(-1, width)
    own_bias = lax.dynamic_slice_in_dim(vectors[8:].reshape(-1), own_index * quarter, quarter, 0)
    before = mm(all_second, w_expand, NN) + own_bias
    active = jnp.maximum(before, 0.0).astype(bf16)
    out_part = mm(active, w_reduce, NT).astype(bf16)
    grad_before = jnp.where(before > 0.0, mm(all_cotan, w_reduce, NN), 0.0)
    before_grad_b = grad_before.astype(bf16)
    second_part = mm(before_grad_b, w_expand, NT).astype(bf16)

    (second_parts,) = exchange(
        3, ("za2a", second_part.reshape(group_count, token_count, width))
    )
    grad_second = jnp.sum(second_parts.astype(jnp.float32), axis=0)
    grad_middle = cotangent + norm_backward(
        grad_second * vectors[5], normed_second, inverse_second
    )
    middle_b = grad_middle.astype(bf16)
    grad_attended = mm(middle_b, w_output, NT).astype(bf16)
    attended_heads = grad_attended.reshape(token_count, HEADS, head_size)
    grad_probs = jnp.einsum(
        "qhd,khd->hqk", attended_heads, value_heads, preferred_element_type=jnp.float32
    )
    grad_value = jnp.einsum(
        "hqk,qhd->khd", probs_b, attended_heads, preferred_element_type=jnp.float32
    )
    delta = jnp.sum(probs * grad_probs, axis=2, keepdims=True)
    grad_scores = (probs * (grad_probs - delta)).astype(bf16)
    grad_query = (
        jnp.einsum("hqk,khd->qhd", grad_scores, key_heads, preferred_element_type=jnp.float32)
        * scale
    )
    grad_key = jnp.einsum(
        "hqk,qhd->khd", grad_scores, query_heads, preferred_element_type=jnp.float32
    )
    query_grad = grad_query.reshape(token_count, width)
    key_grad = grad_key.reshape(token_count, width)
    value_grad = grad_value.reshape(token_count, width)
    query_grad_b = query_grad.astype(bf16)
    key_grad_b = key_grad.astype(bf16)
    value_grad_b = value_grad.astype(bf16)

    ffn_terms = jnp.stack(
        [mm(all_second, before_grad_b, TN).astype(bf16), mm(all_cotan, active, TN).astype(bf16)]
    )
    left, right, ffn_total = exchange(
        4,
        ("za2a", jnp.stack([hidden_first, hidden_first, hidden_first, attended])),
        ("za2a", jnp.stack([query_grad_b, key_grad_b, value_grad_b, middle_b])),
        ("dpscatter", ffn_terms),
    )
    grad_first = (
        mm(query_grad_b, w_query, NT) + mm(key_grad_b, w_key, NT) + mm(value_grad_b, w_value, NT)
    )
    input_grad = grad_middle + norm_backward(grad_first * vectors[0], normed_first, inverse_first)
    small_terms = jnp.stack(
        [
            jnp.sum(grad_first * normed_first, axis=0),
            jnp.sum(grad_first, axis=0),
            jnp.sum(query_grad, axis=0),
            jnp.sum(value_grad, axis=0),
            jnp.sum(grad_middle, axis=0),
            jnp.sum(grad_second * normed_second, axis=0),
            jnp.sum(grad_second, axis=0),
            jnp.sum(cotangent, axis=0),
        ]
    )
    owner_mask = jnp.arange(group_count, dtype=jnp.int32) == own_index
    bias_terms = jnp.where(owner_mask[:, None], jnp.sum(grad_before, axis=0)[None], 0.0)
    vector_terms = jnp.concatenate([small_terms, bias_terms.reshape(-1, width)], axis=0)
    attn_term = mm(left.reshape(-1, width), right.reshape(-1, width), TN).astype(bf16)
    vector_all, attn_total = exchange(5, ("dpag", vector_terms), ("dpscatter", attn_term[None]))
    total_tokens = float(token_count * dp_count * group_count)
    attn_grads = attn_total / total_tokens
    ffn_grads = ffn_total / total_tokens
    attn_next = momentum_rate * attn_momenta + attn_grads
    ffn_next = momentum_rate * ffn_momenta + ffn_grads
    own_next = jnp.concatenate([attn_next, ffn_next], axis=0)
    squares = jnp.sum(own_next * own_next, axis=(1, 2))
    squares = jnp.broadcast_to(jnp.pad(squares, (0, 5))[:, None], (8, 128))

    next_full, square_all, vector_groups, out_parts = exchange(
        6,
        ("dprow", own_next.astype(bf16)),
        ("dpag", squares),
        ("zag", jnp.sum(vector_all, axis=0)),
        ("za2a", out_part.reshape(group_count, token_count, width)),
    )
    outputs = middle + jnp.sum(out_parts.astype(jnp.float32), axis=0) + vectors[7]
    square_plane = jnp.sum(square_all, axis=0)
    own_b = own_next.astype(bf16)
    gram_part = jnp.concatenate([mm(own_b[1], next_full[1], NT), mm(own_b[2], next_full[2], NT)])
    piece = 2 * own_count // group_count
    gram_pieces, square_groups = exchange(
        7,
        ("za2a", gram_part.astype(bf16).reshape(group_count, piece, width)),
        ("zag", square_plane),
    )
    ffn_square = jnp.sum(square_groups, axis=0)[1:3, 0]
    attn_scale = 1.0 / (jnp.sqrt(square_plane[0, 0]) + 1e-07)
    ffn_scale = 1.0 / (jnp.sqrt(ffn_square) + 1e-07)
    piece_scale = jnp.where(own_index < group_count // 2, ffn_scale[0], ffn_scale[1])
    gram_piece = (jnp.sum(gram_pieces.astype(jnp.float32), axis=0) * (piece_scale * piece_scale)).astype(bf16)
    (gram_full,) = exchange(8, (("chain", 2), gram_piece))

    row_start = dp_index * own_count
    attn_unit = next_full[0].astype(jnp.float32) * attn_scale
    attn_unit_b = attn_unit.astype(bf16)
    attn_gram = mm(attn_unit_b, attn_unit_b, NT)
    steps = [newton_schulz_rows(attn_gram, own_next[0] * attn_scale, attn_unit_b, row_start)]
    for i in range(2):
        unit_b = (next_full[1 + i].astype(jnp.float32) * ffn_scale[i]).astype(bf16)
        steps.append(
            newton_schulz_rows(
                gram_full[i].astype(jnp.float32), own_next[1 + i] * ffn_scale[i], unit_b, row_start
            )
        )
    new_attn_weights = attn_weights - muon_rate * steps[0][None]
    new_ffn_weights = ffn_weights - muon_rate * jnp.stack(steps[1:])
    vector_grads = jnp.sum(vector_groups, axis=0) / total_tokens
    new_vector_momenta = momentum_rate * vector_momenta + vector_grads
    mean_square = jnp.mean(new_vector_momenta * new_vector_momenta, axis=1, keepdims=True)
    new_vectors = vectors - vector_rate * new_vector_momenta * lax.rsqrt(mean_square + 1e-06)
    return (
        outputs,
        input_grad,
        attn_grads,
        ffn_grads,
        vector_grads,
        new_attn_weights,
        attn_next,
        new_ffn_weights,
        ffn_next,
        new_vectors,
        new_vector_momenta,
    )


def solution(mesh):
    in_specs = (
        P(("dp", "group"), None),
        P(("dp", "group"), None),
        P(("dp", "group"), None),
        P("group", "dp", None),
        P("group", "dp", None),
        P(None, "dp", "group"),
        P(None, "dp", "group"),
        P(),
        P(),
    )
    out_specs = (
        P(("dp", "group"), None),
        P(("dp", "group"), None),
        P("group", "dp", None),
        P(None, "dp", "group"),
        P(),
        P("group", "dp", None),
        P("group", "dp", None),
        P(None, "dp", "group"),
        P(None, "dp", "group"),
        P(),
        P(),
    )
    return jax.shard_map(
        on_device, mesh=mesh, in_specs=in_specs, out_specs=out_specs, check_vma=False
    )
```

```python
import math

import jax
import jax.numpy as jnp
from jax import lax
from jax.experimental import pallas as pl
from jax.experimental.pallas import tpu as pltpu
from jax.sharding import PartitionSpec as P

HEADS = 12
NS_ITERS = 3


coef_first = 3.4445
coef_second = -4.775
coef_third = 2.0315
momentum_rate = 0.9
muon_rate = 0.8
vector_rate = 0.1


def norm_forward(rows):
    centre = jnp.mean(rows, axis=1, keepdims=True)
    centred = rows - centre
    variance = jnp.mean(centred * centred, axis=1, keepdims=True)
    inverse = lax.rsqrt(variance + 1e-05)
    return (centred * inverse, inverse)


def norm_backward(grad_normed, normed, inverse):
    return inverse * (
        grad_normed
        - jnp.mean(grad_normed, axis=1, keepdims=True)
        - normed * jnp.mean(grad_normed * normed, axis=1, keepdims=True)
    )


def masked_scores(query_heads, key_heads, allowed):
    scores = jnp.einsum("qhd,khd->hqk", query_heads, key_heads, preferred_element_type=jnp.float32)
    return jnp.where(allowed[None], scores, -jnp.inf)


MESH = pl.DeviceIdType.MESH


def flip(index, bits):
    result = index
    for bit in (1, 2, 4):
        if bits & bit:
            result = result + bit - 2 * bit * ((index // bit) % 2)
    return result


def out_struct(kind, x, n_group):
    dtype = x.dtype
    if kind == "zag":
        shape = (n_group,) + x.shape
    elif kind == "za2a":
        shape = x.shape
    elif kind == "dpag":
        shape = (8,) + x.shape
    elif kind == "dprow":
        shape = (x.shape[0], 8 * x.shape[1], x.shape[2])
    elif kind == "dpscatter":
        shape = (x.shape[0], x.shape[1] // 8, x.shape[2])
        dtype = jnp.float32
    else:
        count = kind[1]
        shape = (count, 8 * (n_group // count) * x.shape[0], x.shape[1])
    return jax.ShapeDtypeStruct(shape, dtype)


def scratch_of(kind, x, n_group):
    if kind[0] == "chain":
        return [pltpu.VMEM((n_group,) + x.shape, x.dtype)]
    if kind == "dpscatter":
        count, rows, width = x.shape
        rows = rows // 8
        return [
            pltpu.VMEM((count, 4, rows, width), x.dtype),
            pltpu.VMEM((count, 4, rows, width), x.dtype),
            pltpu.VMEM((count, 4, rows // 2, width), x.dtype),
            pltpu.VMEM((count, 2, rows // 2, width), x.dtype),
            pltpu.VMEM((count, 2, rows // 2, width), x.dtype),
        ]
    return []


def copies_of(kind, x, n_group):
    if kind[0] == "chain":
        return n_group - 1 + 8 * n_group
    if kind == "dprow":
        return 8 * x.shape[0]
    if kind == "dpscatter":
        return 10 * x.shape[0]
    return 7 if kind == "dpag" else n_group - 1


def exchange_kernel(kinds, n_group, scratch_counts, *refs):
    count = len(kinds)
    ins, outs = refs[:count], refs[count : 2 * count]
    send_sem, recv_sem = refs[-2:]
    spare = list(refs[2 * count : -2])
    scratch = []
    for number in scratch_counts:
        scratch.append(spare[:number])
        spare = spare[number:]
    z = lax.axis_index("group")
    d = lax.axis_index("dp")
    z_used = any(kind[0] in ("z", "chain") for kind in kinds)
    dp_used = any(kind[0] in ("d", "chain") for kind in kinds)

    def z_peer(k):
        return lax.rem(z + k, n_group)

    barrier = pltpu.get_barrier_semaphore()
    greeted = 0
    if z_used:
        for k in range(1, n_group):
            pl.semaphore_signal(
                barrier, inc=1, device_id={"group": z_peer(k)}, device_id_type=MESH
            )
            greeted += 1
    if dp_used:
        for k in range(1, 8):
            pl.semaphore_signal(barrier, inc=1, device_id={"dp": flip(d, k)}, device_id_type=MESH)
            greeted += 1
    pl.semaphore_wait(barrier, greeted)

    slot = [0]

    def send(src, dst, device):
        copy = pltpu.make_async_remote_copy(
            src_ref=src,
            dst_ref=dst,
            send_sem=send_sem.at[slot[0]],
            recv_sem=recv_sem.at[slot[0]],
            device_id=device,
            device_id_type=MESH,
        )
        slot[0] += 1
        copy.start()
        return copy

    pending = []
    staged = []

    def spread(src, o, matrix, block, offset, rows):
        first = rows // 32 * 16

        def place(index, part=None):
            start = index * block + offset
            size = rows
            if part is not None:
                start = start + part * first
                size = (first, rows - first)[part]
            return o.at[matrix, pl.ds(pl.multiple_of(start, 16), size), :]

        along_x = send(src, place(d), {"dp": flip(d, 2)})
        along_y = send(src, place(d), {"dp": flip(d, 4)})
        sibling = send(src, place(d), {"dp": flip(d, 1)})
        staged.append((place, along_x, along_y, sibling))

    chained = []
    for kind, x, o, spare in zip(kinds, ins, outs, scratch):
        if kind[0] == "chain":
            copies = [
                send(x, spare[0].at[z], {"group": z_peer(k)}) for k in range(1, n_group)
            ]
            per = n_group // kind[1]
            chained.append((copies, x, o, spare[0], per))
            rows = x.shape[0]
            spread(x, o, z // per, per * rows, lax.rem(z, per) * rows, rows)
    scatters = []
    for kind, x, o, spare in zip(kinds, ins, outs, scratch):
        if kind == "dprow":
            rows = x.shape[1]
            for i in range(x.shape[0]):
                spread(x.at[i], o, i, rows, 0, rows)
        elif kind == "dpscatter":
            rows = x.shape[1] // 8
            for i in range(x.shape[0]):
                copies = []
                for r in (3, 1, 2, 0):
                    start = pl.multiple_of(flip(d, 2 * r + 1) * rows, rows)
                    copies.append(
                        send(
                            x.at[i, pl.ds(start, rows), :],
                            spare[0].at[i, r],
                            {"dp": flip(d, 1)},
                        )
                    )
                scatters.append((i, x, o, rows, spare, copies))
        elif kind == "dpag":
            for k in range(1, 8):
                pending.append(send(x, o.at[d], {"dp": flip(d, k)}))
    if not chained:
        start_z(kinds, ins, outs, z, z_peer, n_group, send, pending)

    for kind, x, o in zip(kinds, ins, outs):
        if kind[0] == "chain":
            per = n_group // kind[1]
            rows = x.shape[0]
            start = pl.multiple_of(d * per * rows + lax.rem(z, per) * rows, 16)
            o[z // per, pl.ds(start, rows), :] = x[...]
        elif kind == "dprow":
            rows = x.shape[1]
            o[:, pl.ds(pl.multiple_of(d * rows, rows), rows), :] = x[...]
        elif kind == "dpag":
            o[d] = x[...]
        elif kind == "zag":
            o[z] = x[...]
        elif kind == "za2a":
            o[z] = x[z]

    for copies, x, o, held, per in chained:
        rows = x.shape[0]
        for k in range(1, n_group):
            copies[k - 1].wait_recv()
            origin = lax.rem(z + n_group - k, n_group)
            offset = lax.rem(origin, per) * rows
            spread(held.at[origin], o, origin // per, per * rows, offset, rows)
            start = pl.multiple_of(d * per * rows + offset, 16)
            o[origin // per, pl.ds(start, rows), :] = held[origin]
    if chained:
        start_z(kinds, ins, outs, z, z_peer, n_group, send, pending)

    second = []
    for place, along_x, along_y, sibling in staged:
        along_x.wait_recv()
        from_x = flip(d, 2)
        to_y = send(place(from_x, 0), place(from_x, 0), {"dp": flip(d, 4)})
        share_x = send(place(from_x), place(from_x), {"dp": flip(d, 1)})
        along_y.wait_recv()
        from_y = flip(d, 4)
        to_x = send(place(from_y, 1), place(from_y, 1), {"dp": flip(d, 2)})
        share_y = send(place(from_y), place(from_y), {"dp": flip(d, 1)})
        second.append((place, (along_x, along_y, to_y, to_x), (sibling, share_x, share_y)))
    third = []
    for place, links, shares in second:
        links[2].wait_recv()
        links[3].wait_recv()
        far = flip(d, 6)
        third.append(send(place(far), place(far), {"dp": flip(d, 1)}))

    wide = jnp.float32
    level = []
    for i, x, o, rows, spare, copies in scatters:
        near, total, recv_b, recv_c, part = spare
        half = rows // 2
        low, high = pl.ds(0, half), pl.ds(half, half)
        for r, copy in zip((3, 1, 2, 0), copies):
            copy.wait_recv()
            start = pl.multiple_of(flip(d, 2 * r) * rows, rows)
            own = x[i, pl.ds(start, rows), :].astype(wide)
            total[i, r] = (own + near[i, r].astype(wide)).astype(total.dtype)
        to_x = {"dp": flip(d, 2)}
        to_y = {"dp": flip(d, 4)}
        moved = [
            send(total.at[i, 3, low], recv_b.at[i, 1], to_x),
            send(total.at[i, 3, high], recv_b.at[i, 3], to_y),
            send(total.at[i, 1, low], recv_b.at[i, 0], to_x),
            send(total.at[i, 2, high], recv_b.at[i, 2], to_y),
        ]
        level.append(moved)
    last = []
    for (i, x, o, rows, spare, copies), moved in zip(scatters, level):
        near, total, recv_b, recv_c, part = spare
        half = rows // 2
        low, high = pl.ds(0, half), pl.ds(half, half)
        moved[0].wait_recv()
        part[i, 0] = (
            total[i, 2, low].astype(wide) + recv_b[i, 1].astype(wide)
        ).astype(part.dtype)
        moved[1].wait_recv()
        part[i, 1] = (
            total[i, 1, high].astype(wide) + recv_b[i, 3].astype(wide)
        ).astype(part.dtype)
        last.append(
            (
                send(part.at[i, 0], recv_c.at[i, 0], {"dp": flip(d, 4)}),
                send(part.at[i, 1], recv_c.at[i, 1], {"dp": flip(d, 2)}),
            )
        )
    for (i, x, o, rows, spare, copies), moved, ends in zip(scatters, level, last):
        near, total, recv_b, recv_c, part = spare
        half = rows // 2
        low, high = pl.ds(0, half), pl.ds(half, half)
        moved[2].wait_recv()
        moved[3].wait_recv()
        ends[0].wait_recv()
        o[i, low, :] = (
            total[i, 0, low].astype(wide) + recv_b[i, 0].astype(wide) + recv_c[i, 0].astype(wide)
        )
        ends[1].wait_recv()
        o[i, high, :] = (
            total[i, 0, high].astype(wide) + recv_b[i, 2].astype(wide) + recv_c[i, 1].astype(wide)
        )
        for copy in (*copies, *moved, *ends):
            copy.wait_send()

    for copies, *_ in chained:
        for copy in copies:
            copy.wait_send()
    for place, links, shares in second:
        for copy in shares:
            copy.wait()
        for copy in links:
            copy.wait_send()
    for copy in third:
        copy.wait()
    for copy in pending:
        copy.wait()


def start_z(kinds, ins, outs, z, z_peer, n_group, send, pending):
    for kind, x, o in zip(kinds, ins, outs):
        for k in range(1, n_group):
            if kind == "zag":
                pending.append(send(x, o.at[z], {"group": z_peer(k)}))
            elif kind == "za2a":
                pending.append(send(x.at[z_peer(k)], o.at[z], {"group": z_peer(k)}))


def exchange(collective_id, *pairs):
    n_group = lax.axis_size("group")
    kinds = tuple(kind for kind, _ in pairs)
    arrays = [x for _, x in pairs]
    if lax.axis_size("dp") != 8:
        results = []
        for kind, x in pairs:
            if kind == "zag":
                results.append(lax.all_gather(x, "group", axis=0))
            elif kind == "za2a":
                results.append(lax.all_to_all(x, "group", 0, 0))
            elif kind == "dpag":
                results.append(lax.all_gather(x, "dp", axis=0))
            elif kind == "dprow":
                results.append(lax.all_gather(x, "dp", axis=1, tiled=True))
            elif kind == "dpscatter":
                wide = x.astype(jnp.float32)
                results.append(lax.psum_scatter(wide, "dp", scatter_dimension=1, tiled=True))
            else:
                held = lax.all_gather(x, "group", axis=0).reshape(kind[1], -1, x.shape[1])
                results.append(lax.all_gather(held, "dp", axis=1, tiled=True))
        return results
    copies = sum(copies_of(kind, x, n_group) for kind, x in pairs)
    scratch = [scratch_of(kind, x, n_group) for kind, x in pairs]
    scratch_counts = tuple(len(shapes) for shapes in scratch)
    return pl.pallas_call(
        lambda *refs: exchange_kernel(kinds, n_group, scratch_counts, *refs),
        out_shape=[out_struct(kind, x, n_group) for kind, x in pairs],
        in_specs=[pl.BlockSpec(memory_space=pltpu.VMEM)] * len(kinds),
        out_specs=[pl.BlockSpec(memory_space=pltpu.VMEM)] * len(kinds),
        scratch_shapes=[
            *[shape for shapes in scratch for shape in shapes],
            pltpu.SemaphoreType.DMA((copies,)),
            pltpu.SemaphoreType.DMA((copies,)),
        ],
        compiler_params=pltpu.CompilerParams(collective_id=collective_id, has_side_effects=True),
        name=f"exchange_{collective_id}",
    )(*arrays)


def mm(left, right, dims):
    return lax.dot_general(left, right, (dims, ((), ())), preferred_element_type=jnp.float32)


NN = ((1,), (0,))
NT = ((1,), (1,))
TN = ((0,), (0,))


def newton_schulz_rows(gram, own_rows, whole_b, row_start):
    rows = own_rows.shape[0]
    lead = 1.0
    spread = None
    for iteration in range(NS_ITERS - 1):
        gram_b = gram.astype(jnp.bfloat16)
        mixed = coef_second * gram + coef_third * mm(gram_b, gram_b, NN)
        mixed_b = mixed.astype(jnp.bfloat16)
        half = coef_first * gram + mm(mixed_b, gram_b, NN)
        gram = coef_first * half + mm(half.astype(jnp.bfloat16), mixed_b, NN)
        mine = lax.dynamic_slice_in_dim(mixed, row_start, rows, 0)
        if spread is None:
            spread = mine
        else:
            product = mm(spread.astype(jnp.bfloat16), mixed_b, NN)
            spread = coef_first * spread + lead * mine + product
        lead = lead * coef_first
    gram_b = gram.astype(jnp.bfloat16)
    once = lead * lax.dynamic_slice_in_dim(gram, row_start, rows, 0) + mm(
        spread.astype(jnp.bfloat16), gram_b, NN
    )
    twice = mm(once.astype(jnp.bfloat16), gram_b, NN)
    spread = coef_first * spread + coef_second * once + coef_third * twice
    lead = lead * coef_first
    return lead * own_rows + mm(spread.astype(jnp.bfloat16), whole_b, NN)


def on_device(
    inputs,
    cotangent,
    lengths,
    attn_weights,
    attn_momenta,
    ffn_weights,
    ffn_momenta,
    vectors,
    vector_momenta,
):
    group_count = lax.axis_size("group")
    dp_count = lax.axis_size("dp")
    own_index = lax.axis_index("group")
    dp_index = lax.axis_index("dp")
    token_count, width = inputs.shape
    own_count = attn_weights.shape[1]
    quarter = ffn_weights.shape[2]
    head_size = width // HEADS
    scale = 1.0 / math.sqrt(head_size)
    bf16 = jnp.bfloat16

    own_attn = attn_weights.astype(bf16)
    own_ffn = ffn_weights.astype(bf16)
    cotan_b = cotangent.astype(bf16)
    attn_full, all_cotan = exchange(0, (("chain", group_count), own_attn[0]), ("zag", cotan_b))
    w_query, w_key, w_value, w_output = [attn_full[i] for i in range(4)]
    all_cotan = all_cotan.reshape(-1, width)

    positions = jnp.arange(token_count, dtype=jnp.int32)
    seq_ends = jnp.cumsum(lengths[0])
    segment = jnp.sum((positions[:, None] >= seq_ends[None, :]).astype(jnp.int32), axis=1)
    allowed = (segment[:, None] == segment[None, :]) & (positions[None, :] <= positions[:, None])
    normed_first, inverse_first = norm_forward(inputs)
    hidden_first = (normed_first * vectors[0] + vectors[1]).astype(bf16)
    query = ((mm(hidden_first, w_query, NN) + vectors[2]) * scale).astype(bf16)
    keyed = mm(hidden_first, w_key, NN).astype(bf16)
    valued = (mm(hidden_first, w_value, NN) + vectors[3]).astype(bf16)
    query_heads = query.reshape(token_count, HEADS, head_size)
    key_heads = keyed.reshape(token_count, HEADS, head_size)
    value_heads = valued.reshape(token_count, HEADS, head_size)
    scores = masked_scores(query_heads, key_heads, allowed)
    highest = jnp.max(scores, axis=2, keepdims=True)
    log_total = highest + jnp.log(jnp.sum(jnp.exp(scores - highest), axis=2, keepdims=True))
    probs = jnp.exp(scores - log_total)
    probs_b = probs.astype(bf16)
    attended = jnp.einsum("hqk,khd->qhd", probs_b, value_heads, preferred_element_type=jnp.float32)
    attended = attended.reshape(token_count, width).astype(bf16)
    middle = inputs + mm(attended, w_output, NN) + vectors[4]
    normed_second, inverse_second = norm_forward(middle)
    hidden_second = (normed_second * vectors[5] + vectors[6]).astype(bf16)

    all_second, ffn_full = exchange(2, ("zag", hidden_second), ("dprow", own_ffn))
    w_expand, w_reduce = ffn_full[0], ffn_full[1]
    all_second = all_second.reshape(-1, width)
    own_bias = lax.dynamic_slice_in_dim(vectors[8:].reshape(-1), own_index * quarter, quarter, 0)
    before = mm(all_second, w_expand, NN) + own_bias
    active = jnp.maximum(before, 0.0).astype(bf16)
    out_part = mm(active, w_reduce, NT).astype(bf16)
    grad_before = jnp.where(before > 0.0, mm(all_cotan, w_reduce, NN), 0.0)
    before_grad_b = grad_before.astype(bf16)
    second_part = mm(before_grad_b, w_expand, NT).astype(bf16)

    ffn_terms = jnp.stack(
        [mm(all_second, before_grad_b, TN).astype(bf16), mm(all_cotan, active, TN).astype(bf16)]
    )
    second_parts, ffn_total = exchange(
        3,
        ("za2a", second_part.reshape(group_count, token_count, width)),
        ("dpscatter", ffn_terms),
    )
    grad_second = jnp.sum(second_parts.astype(jnp.float32), axis=0)
    grad_middle = cotangent + norm_backward(
        grad_second * vectors[5], normed_second, inverse_second
    )
    middle_b = grad_middle.astype(bf16)
    grad_attended = mm(middle_b, w_output, NT).astype(bf16)
    attended_heads = grad_attended.reshape(token_count, HEADS, head_size)
    grad_probs = jnp.einsum(
        "qhd,khd->hqk", attended_heads, value_heads, preferred_element_type=jnp.float32
    )
    grad_value = jnp.einsum(
        "hqk,qhd->khd", probs_b, attended_heads, preferred_element_type=jnp.float32
    )
    delta = jnp.sum(probs * grad_probs, axis=2, keepdims=True)
    grad_scores = (probs * (grad_probs - delta)).astype(bf16)
    grad_query = (
        jnp.einsum("hqk,khd->qhd", grad_scores, key_heads, preferred_element_type=jnp.float32)
        * scale
    )
    grad_key = jnp.einsum(
        "hqk,qhd->khd", grad_scores, query_heads, preferred_element_type=jnp.float32
    )
    query_grad = grad_query.reshape(token_count, width)
    key_grad = grad_key.reshape(token_count, width)
    value_grad = grad_value.reshape(token_count, width)
    query_grad_b = query_grad.astype(bf16)
    key_grad_b = key_grad.astype(bf16)
    value_grad_b = value_grad.astype(bf16)

    grad_first = (
        mm(query_grad_b, w_query, NT) + mm(key_grad_b, w_key, NT) + mm(value_grad_b, w_value, NT)
    )
    input_grad = grad_middle + norm_backward(grad_first * vectors[0], normed_first, inverse_first)
    small_terms = jnp.stack(
        [
            jnp.sum(grad_first * normed_first, axis=0),
            jnp.sum(grad_first, axis=0),
            jnp.sum(query_grad, axis=0),
            jnp.sum(value_grad, axis=0),
            jnp.sum(grad_middle, axis=0),
            jnp.sum(grad_second * normed_second, axis=0),
            jnp.sum(grad_second, axis=0),
            jnp.sum(cotangent, axis=0),
        ]
    )
    owner_mask = jnp.arange(group_count, dtype=jnp.int32) == own_index
    bias_terms = jnp.where(owner_mask[:, None], jnp.sum(grad_before, axis=0)[None], 0.0)
    vector_terms = jnp.concatenate([small_terms, bias_terms.reshape(-1, width)], axis=0)
    attn_terms = jnp.stack(
        [
            mm(hidden_first, query_grad_b, TN).astype(bf16),
            mm(hidden_first, key_grad_b, TN).astype(bf16),
            mm(hidden_first, value_grad_b, TN).astype(bf16),
            mm(attended, middle_b, TN).astype(bf16),
        ]
    )
    attn_sums, vector_all, out_parts = exchange(
        4,
        ("dpscatter", attn_terms),
        ("dpag", vector_terms),
        ("za2a", out_part.reshape(group_count, token_count, width)),
    )
    outputs = middle + jnp.sum(out_parts.astype(jnp.float32), axis=0) + vectors[7]
    attn_parts, vector_groups = exchange(
        5, ("za2a", attn_sums.astype(bf16)), ("zag", jnp.sum(vector_all, axis=0))
    )
    attn_total = jnp.sum(attn_parts.astype(jnp.float32), axis=0)[None]
    total_tokens = float(token_count * dp_count * group_count)
    attn_grads = attn_total / total_tokens
    ffn_grads = ffn_total / total_tokens
    attn_next = momentum_rate * attn_momenta + attn_grads
    ffn_next = momentum_rate * ffn_momenta + ffn_grads
    own_next = jnp.concatenate([attn_next, ffn_next], axis=0)
    squares = jnp.sum(own_next * own_next, axis=(1, 2))
    squares = jnp.broadcast_to(jnp.pad(squares, (0, 5))[:, None], (8, 128))

    next_full, square_all = exchange(6, ("dprow", own_next.astype(bf16)), ("dpag", squares))
    square_plane = jnp.sum(square_all, axis=0)
    own_b = own_next.astype(bf16)
    gram_part = jnp.concatenate([mm(own_b[1], next_full[1], NT), mm(own_b[2], next_full[2], NT)])
    piece = 2 * own_count // group_count
    gram_pieces, square_groups = exchange(
        7,
        ("za2a", gram_part.astype(bf16).reshape(group_count, piece, width)),
        ("zag", square_plane),
    )
    ffn_square = jnp.sum(square_groups, axis=0)[1:3, 0]
    attn_scale = 1.0 / (jnp.sqrt(square_plane[0, 0]) + 1e-07)
    ffn_scale = 1.0 / (jnp.sqrt(ffn_square) + 1e-07)
    piece_scale = jnp.where(own_index < group_count // 2, ffn_scale[0], ffn_scale[1])
    gram_piece = (jnp.sum(gram_pieces.astype(jnp.float32), axis=0) * (piece_scale * piece_scale)).astype(bf16)
    (gram_full,) = exchange(8, (("chain", 2), gram_piece))

    row_start = dp_index * own_count
    attn_unit = next_full[0].astype(jnp.float32) * attn_scale
    attn_unit_b = attn_unit.astype(bf16)
    attn_gram = mm(attn_unit_b, attn_unit_b, NT)
    steps = [newton_schulz_rows(attn_gram, own_next[0] * attn_scale, attn_unit_b, row_start)]
    for i in range(2):
        unit_b = (next_full[1 + i].astype(jnp.float32) * ffn_scale[i]).astype(bf16)
        steps.append(
            newton_schulz_rows(
                gram_full[i].astype(jnp.float32), own_next[1 + i] * ffn_scale[i], unit_b, row_start
            )
        )
    new_attn_weights = attn_weights - muon_rate * steps[0][None]
    new_ffn_weights = ffn_weights - muon_rate * jnp.stack(steps[1:])
    vector_grads = jnp.sum(vector_groups, axis=0) / total_tokens
    new_vector_momenta = momentum_rate * vector_momenta + vector_grads
    mean_square = jnp.mean(new_vector_momenta * new_vector_momenta, axis=1, keepdims=True)
    new_vectors = vectors - vector_rate * new_vector_momenta * lax.rsqrt(mean_square + 1e-06)
    return (
        outputs,
        input_grad,
        attn_grads,
        ffn_grads,
        vector_grads,
        new_attn_weights,
        attn_next,
        new_ffn_weights,
        ffn_next,
        new_vectors,
        new_vector_momenta,
    )


def solution(mesh):
    in_specs = (
        P(("dp", "group"), None),
        P(("dp", "group"), None),
        P(("dp", "group"), None),
        P("group", "dp", None),
        P("group", "dp", None),
        P(None, "dp", "group"),
        P(None, "dp", "group"),
        P(),
        P(),
    )
    out_specs = (
        P(("dp", "group"), None),
        P(("dp", "group"), None),
        P("group", "dp", None),
        P(None, "dp", "group"),
        P(),
        P("group", "dp", None),
        P("group", "dp", None),
        P(None, "dp", "group"),
        P(None, "dp", "group"),
        P(),
        P(),
    )
    return jax.shard_map(
        on_device, mesh=mesh, in_specs=in_specs, out_specs=out_specs, check_vma=False
    )
```

```python
import math

import jax
import jax.numpy as jnp
from jax import lax
from jax.experimental import pallas as pl
from jax.experimental.pallas import tpu as pltpu
from jax.sharding import PartitionSpec as P

HEADS = 12
NS_ITERS = 3


coef_first = 3.4445
coef_second = -4.775
coef_third = 2.0315
momentum_rate = 0.9
muon_rate = 0.8
vector_rate = 0.1


def norm_forward(rows):
    centre = jnp.mean(rows, axis=1, keepdims=True)
    centred = rows - centre
    variance = jnp.mean(centred * centred, axis=1, keepdims=True)
    inverse = lax.rsqrt(variance + 1e-05)
    return (centred * inverse, inverse)


def norm_backward(grad_normed, normed, inverse):
    return inverse * (
        grad_normed
        - jnp.mean(grad_normed, axis=1, keepdims=True)
        - normed * jnp.mean(grad_normed * normed, axis=1, keepdims=True)
    )


def masked_scores(query_heads, key_heads, allowed):
    scores = jnp.einsum("qhd,khd->hqk", query_heads, key_heads, preferred_element_type=jnp.float32)
    return jnp.where(allowed[None], scores, -jnp.inf)


MESH = pl.DeviceIdType.MESH


def flip(index, bits):
    result = index
    for bit in (1, 2, 4):
        if bits & bit:
            result = result + bit - 2 * bit * ((index // bit) % 2)
    return result


def out_struct(kind, x, n_group):
    dtype = x.dtype
    if kind == "zag":
        shape = (n_group,) + x.shape
    elif kind == "za2a":
        shape = x.shape
    elif kind == "dpag":
        shape = (8,) + x.shape
    elif kind == "dprow":
        shape = (x.shape[0], 8 * x.shape[1], x.shape[2])
    elif kind == "dpscatter":
        shape = (x.shape[0], x.shape[1] // 8, x.shape[2])
        dtype = jnp.float32
    else:
        count = kind[1]
        shape = (count, 8 * (n_group // count) * x.shape[0], x.shape[1])
    return jax.ShapeDtypeStruct(shape, dtype)


def scratch_of(kind, x, n_group):
    if kind[0] == "chain":
        return [pltpu.VMEM((n_group,) + x.shape, x.dtype)]
    if kind == "dpscatter":
        count, rows, width = x.shape
        rows = rows // 8
        return [
            pltpu.VMEM((count, 4, rows, width), x.dtype),
            pltpu.VMEM((count, 4, rows, width), x.dtype),
            pltpu.VMEM((count, 4, rows // 2, width), x.dtype),
            pltpu.VMEM((count, 2, rows // 2, width), x.dtype),
            pltpu.VMEM((count, 2, rows // 2, width), x.dtype),
        ]
    return []


def copies_of(kind, x, n_group):
    if kind[0] == "chain":
        return n_group - 1 + 8 * n_group
    if kind == "dprow":
        return 8 * x.shape[0]
    if kind == "dpscatter":
        return 10 * x.shape[0]
    return 7 if kind == "dpag" else n_group - 1


def exchange_kernel(kinds, n_group, scratch_counts, *refs):
    count = len(kinds)
    ins, outs = refs[:count], refs[count : 2 * count]
    send_sem, recv_sem = refs[-2:]
    spare = list(refs[2 * count : -2])
    scratch = []
    for number in scratch_counts:
        scratch.append(spare[:number])
        spare = spare[number:]
    z = lax.axis_index("group")
    d = lax.axis_index("dp")
    z_used = any(kind[0] in ("z", "chain") for kind in kinds)
    dp_used = any(kind[0] in ("d", "chain") for kind in kinds)

    def z_peer(k):
        return lax.rem(z + k, n_group)

    barrier = pltpu.get_barrier_semaphore()
    greeted = 0
    if z_used:
        for k in range(1, n_group):
            pl.semaphore_signal(
                barrier, inc=1, device_id={"group": z_peer(k)}, device_id_type=MESH
            )
            greeted += 1
    if dp_used:
        for k in range(1, 8):
            pl.semaphore_signal(barrier, inc=1, device_id={"dp": flip(d, k)}, device_id_type=MESH)
            greeted += 1
    pl.semaphore_wait(barrier, greeted)

    slot = [0]

    def send(src, dst, device):
        copy = pltpu.make_async_remote_copy(
            src_ref=src,
            dst_ref=dst,
            send_sem=send_sem.at[slot[0]],
            recv_sem=recv_sem.at[slot[0]],
            device_id=device,
            device_id_type=MESH,
        )
        slot[0] += 1
        copy.start()
        return copy

    pending = []
    staged = []

    def spread(src, o, matrix, block, offset, rows):
        first = rows // 32 * 16

        def place(index, part=None):
            start = index * block + offset
            size = rows
            if part is not None:
                start = start + part * first
                size = (first, rows - first)[part]
            return o.at[matrix, pl.ds(pl.multiple_of(start, 16), size), :]

        along_x = send(src, place(d), {"dp": flip(d, 2)})
        along_y = send(src, place(d), {"dp": flip(d, 4)})
        sibling = send(src, place(d), {"dp": flip(d, 1)})
        staged.append((place, along_x, along_y, sibling))

    chained = []
    for kind, x, o, spare in zip(kinds, ins, outs, scratch):
        if kind[0] == "chain":
            copies = [
                send(x, spare[0].at[z], {"group": z_peer(k)}) for k in range(1, n_group)
            ]
            per = n_group // kind[1]
            chained.append((copies, x, o, spare[0], per))
            rows = x.shape[0]
            spread(x, o, z // per, per * rows, lax.rem(z, per) * rows, rows)
    scatters = []
    for kind, x, o, spare in zip(kinds, ins, outs, scratch):
        if kind == "dprow":
            rows = x.shape[1]
            for i in range(x.shape[0]):
                spread(x.at[i], o, i, rows, 0, rows)
        elif kind == "dpscatter":
            rows = x.shape[1] // 8
            for i in range(x.shape[0]):
                copies = []
                for r in (3, 1, 2, 0):
                    start = pl.multiple_of(flip(d, 2 * r + 1) * rows, rows)
                    copies.append(
                        send(
                            x.at[i, pl.ds(start, rows), :],
                            spare[0].at[i, r],
                            {"dp": flip(d, 1)},
                        )
                    )
                scatters.append((i, x, o, rows, spare, copies))
        elif kind == "dpag":
            for k in range(1, 8):
                pending.append(send(x, o.at[d], {"dp": flip(d, k)}))
    if not chained:
        start_z(kinds, ins, outs, z, z_peer, n_group, send, pending)

    for kind, x, o in zip(kinds, ins, outs):
        if kind[0] == "chain":
            per = n_group // kind[1]
            rows = x.shape[0]
            start = pl.multiple_of(d * per * rows + lax.rem(z, per) * rows, 16)
            o[z // per, pl.ds(start, rows), :] = x[...]
        elif kind == "dprow":
            rows = x.shape[1]
            o[:, pl.ds(pl.multiple_of(d * rows, rows), rows), :] = x[...]
        elif kind == "dpag":
            o[d] = x[...]
        elif kind == "zag":
            o[z] = x[...]
        elif kind == "za2a":
            o[z] = x[z]

    for copies, x, o, held, per in chained:
        rows = x.shape[0]
        for k in range(1, n_group):
            copies[k - 1].wait_recv()
            origin = lax.rem(z + n_group - k, n_group)
            offset = lax.rem(origin, per) * rows
            spread(held.at[origin], o, origin // per, per * rows, offset, rows)
            start = pl.multiple_of(d * per * rows + offset, 16)
            o[origin // per, pl.ds(start, rows), :] = held[origin]
    if chained:
        start_z(kinds, ins, outs, z, z_peer, n_group, send, pending)

    second = []
    for place, along_x, along_y, sibling in staged:
        along_x.wait_recv()
        from_x = flip(d, 2)
        to_y = send(place(from_x, 0), place(from_x, 0), {"dp": flip(d, 4)})
        share_x = send(place(from_x), place(from_x), {"dp": flip(d, 1)})
        along_y.wait_recv()
        from_y = flip(d, 4)
        to_x = send(place(from_y, 1), place(from_y, 1), {"dp": flip(d, 2)})
        share_y = send(place(from_y), place(from_y), {"dp": flip(d, 1)})
        second.append((place, (along_x, along_y, to_y, to_x), (sibling, share_x, share_y)))
    third = []
    for place, links, shares in second:
        links[2].wait_recv()
        links[3].wait_recv()
        far = flip(d, 6)
        third.append(send(place(far), place(far), {"dp": flip(d, 1)}))

    wide = jnp.float32
    level = []
    for i, x, o, rows, spare, copies in scatters:
        near, total, recv_b, recv_c, part = spare
        half = rows // 2
        low, high = pl.ds(0, half), pl.ds(half, half)
        for r, copy in zip((3, 1, 2, 0), copies):
            copy.wait_recv()
            start = pl.multiple_of(flip(d, 2 * r) * rows, rows)
            own = x[i, pl.ds(start, rows), :].astype(wide)
            total[i, r] = (own + near[i, r].astype(wide)).astype(total.dtype)
        to_x = {"dp": flip(d, 2)}
        to_y = {"dp": flip(d, 4)}
        moved = [
            send(total.at[i, 3, low], recv_b.at[i, 1], to_x),
            send(total.at[i, 3, high], recv_b.at[i, 3], to_y),
            send(total.at[i, 1, low], recv_b.at[i, 0], to_x),
            send(total.at[i, 2, high], recv_b.at[i, 2], to_y),
        ]
        level.append(moved)
    last = []
    for (i, x, o, rows, spare, copies), moved in zip(scatters, level):
        near, total, recv_b, recv_c, part = spare
        half = rows // 2
        low, high = pl.ds(0, half), pl.ds(half, half)
        moved[0].wait_recv()
        part[i, 0] = (
            total[i, 2, low].astype(wide) + recv_b[i, 1].astype(wide)
        ).astype(part.dtype)
        moved[1].wait_recv()
        part[i, 1] = (
            total[i, 1, high].astype(wide) + recv_b[i, 3].astype(wide)
        ).astype(part.dtype)
        last.append(
            (
                send(part.at[i, 0], recv_c.at[i, 0], {"dp": flip(d, 4)}),
                send(part.at[i, 1], recv_c.at[i, 1], {"dp": flip(d, 2)}),
            )
        )
    for (i, x, o, rows, spare, copies), moved, ends in zip(scatters, level, last):
        near, total, recv_b, recv_c, part = spare
        half = rows // 2
        low, high = pl.ds(0, half), pl.ds(half, half)
        moved[2].wait_recv()
        moved[3].wait_recv()
        ends[0].wait_recv()
        o[i, low, :] = (
            total[i, 0, low].astype(wide) + recv_b[i, 0].astype(wide) + recv_c[i, 0].astype(wide)
        )
        ends[1].wait_recv()
        o[i, high, :] = (
            total[i, 0, high].astype(wide) + recv_b[i, 2].astype(wide) + recv_c[i, 1].astype(wide)
        )
        for copy in (*copies, *moved, *ends):
            copy.wait_send()

    for copies, *_ in chained:
        for copy in copies:
            copy.wait_send()
    for place, links, shares in second:
        for copy in shares:
            copy.wait()
        for copy in links:
            copy.wait_send()
    for copy in third:
        copy.wait()
    for copy in pending:
        copy.wait()


def start_z(kinds, ins, outs, z, z_peer, n_group, send, pending):
    for kind, x, o in zip(kinds, ins, outs):
        for k in range(1, n_group):
            if kind == "zag":
                pending.append(send(x, o.at[z], {"group": z_peer(k)}))
            elif kind == "za2a":
                pending.append(send(x.at[z_peer(k)], o.at[z], {"group": z_peer(k)}))


def exchange(collective_id, *pairs):
    n_group = lax.axis_size("group")
    kinds = tuple(kind for kind, _ in pairs)
    arrays = [x for _, x in pairs]
    if lax.axis_size("dp") != 8:
        results = []
        for kind, x in pairs:
            if kind == "zag":
                results.append(lax.all_gather(x, "group", axis=0))
            elif kind == "za2a":
                results.append(lax.all_to_all(x, "group", 0, 0))
            elif kind == "dpag":
                results.append(lax.all_gather(x, "dp", axis=0))
            elif kind == "dprow":
                results.append(lax.all_gather(x, "dp", axis=1, tiled=True))
            elif kind == "dpscatter":
                wide = x.astype(jnp.float32)
                results.append(lax.psum_scatter(wide, "dp", scatter_dimension=1, tiled=True))
            else:
                held = lax.all_gather(x, "group", axis=0).reshape(kind[1], -1, x.shape[1])
                results.append(lax.all_gather(held, "dp", axis=1, tiled=True))
        return results
    copies = sum(copies_of(kind, x, n_group) for kind, x in pairs)
    scratch = [scratch_of(kind, x, n_group) for kind, x in pairs]
    scratch_counts = tuple(len(shapes) for shapes in scratch)
    return pl.pallas_call(
        lambda *refs: exchange_kernel(kinds, n_group, scratch_counts, *refs),
        out_shape=[out_struct(kind, x, n_group) for kind, x in pairs],
        in_specs=[pl.BlockSpec(memory_space=pltpu.VMEM)] * len(kinds),
        out_specs=[pl.BlockSpec(memory_space=pltpu.VMEM)] * len(kinds),
        scratch_shapes=[
            *[shape for shapes in scratch for shape in shapes],
            pltpu.SemaphoreType.DMA((copies,)),
            pltpu.SemaphoreType.DMA((copies,)),
        ],
        compiler_params=pltpu.CompilerParams(collective_id=collective_id, has_side_effects=True),
        name=f"exchange_{collective_id}",
    )(*arrays)


def mm(left, right, dims):
    return lax.dot_general(left, right, (dims, ((), ())), preferred_element_type=jnp.float32)


NN = ((1,), (0,))
NT = ((1,), (1,))
TN = ((0,), (0,))


def newton_schulz_rows(gram, own_rows, whole_b, row_start):
    rows = own_rows.shape[0]
    lead = 1.0
    spread = None
    for iteration in range(NS_ITERS - 1):
        gram_b = gram.astype(jnp.bfloat16)
        mixed = coef_second * gram + coef_third * mm(gram_b, gram_b, NN)
        mixed_b = mixed.astype(jnp.bfloat16)
        half = coef_first * gram + mm(mixed_b, gram_b, NN)
        gram = coef_first * half + mm(half.astype(jnp.bfloat16), mixed_b, NN)
        mine = lax.dynamic_slice_in_dim(mixed, row_start, rows, 0)
        if spread is None:
            spread = mine
        else:
            product = mm(spread.astype(jnp.bfloat16), mixed_b, NN)
            spread = coef_first * spread + lead * mine + product
        lead = lead * coef_first
    gram_b = gram.astype(jnp.bfloat16)
    once = lead * lax.dynamic_slice_in_dim(gram, row_start, rows, 0) + mm(
        spread.astype(jnp.bfloat16), gram_b, NN
    )
    twice = mm(once.astype(jnp.bfloat16), gram_b, NN)
    spread = coef_first * spread + coef_second * once + coef_third * twice
    lead = lead * coef_first
    return lead * own_rows + mm(spread.astype(jnp.bfloat16), whole_b, NN)


def on_device(
    inputs,
    cotangent,
    lengths,
    attn_weights,
    attn_momenta,
    ffn_weights,
    ffn_momenta,
    vectors,
    vector_momenta,
):
    group_count = lax.axis_size("group")
    dp_count = lax.axis_size("dp")
    own_index = lax.axis_index("group")
    dp_index = lax.axis_index("dp")
    token_count, width = inputs.shape
    own_count = attn_weights.shape[1]
    quarter = ffn_weights.shape[2]
    head_size = width // HEADS
    scale = 1.0 / math.sqrt(head_size)
    bf16 = jnp.bfloat16

    own_attn = attn_weights.astype(bf16)
    own_ffn = ffn_weights.astype(bf16)
    cotan_b = cotangent.astype(bf16)
    attn_full, ffn_full, all_cotan = exchange(
        0, (("chain", 4), own_attn[0]), ("dprow", own_ffn), ("zag", cotan_b)
    )
    w_query, w_key, w_value, w_output = [attn_full[i] for i in range(4)]
    w_expand, w_reduce = [ffn_full[i] for i in range(2)]
    all_cotan = all_cotan.reshape(-1, width)

    positions = jnp.arange(token_count, dtype=jnp.int32)
    seq_ends = jnp.cumsum(lengths[0])
    segment = jnp.sum((positions[:, None] >= seq_ends[None, :]).astype(jnp.int32), axis=1)
    allowed = (segment[:, None] == segment[None, :]) & (positions[None, :] <= positions[:, None])
    normed_first, inverse_first = norm_forward(inputs)
    hidden_first = (normed_first * vectors[0] + vectors[1]).astype(bf16)
    query = ((mm(hidden_first, w_query, NN) + vectors[2]) * scale).astype(bf16)
    keyed = mm(hidden_first, w_key, NN).astype(bf16)
    valued = (mm(hidden_first, w_value, NN) + vectors[3]).astype(bf16)
    query_heads = query.reshape(token_count, HEADS, head_size)
    key_heads = keyed.reshape(token_count, HEADS, head_size)
    value_heads = valued.reshape(token_count, HEADS, head_size)
    scores = masked_scores(query_heads, key_heads, allowed)
    highest = jnp.max(scores, axis=2, keepdims=True)
    log_total = highest + jnp.log(jnp.sum(jnp.exp(scores - highest), axis=2, keepdims=True))
    probs = jnp.exp(scores - log_total)
    probs_b = probs.astype(bf16)
    attended = jnp.einsum("hqk,khd->qhd", probs_b, value_heads, preferred_element_type=jnp.float32)
    attended = attended.reshape(token_count, width).astype(bf16)
    middle = inputs + mm(attended, w_output, NN) + vectors[4]
    normed_second, inverse_second = norm_forward(middle)
    hidden_second = (normed_second * vectors[5] + vectors[6]).astype(bf16)

    (all_second,) = exchange(2, ("zag", hidden_second))
    all_second = all_second.reshape(-1, width)
    own_bias = lax.dynamic_slice_in_dim(vectors[8:].reshape(-1), own_index * quarter, quarter, 0)
    before = mm(all_second, w_expand, NN) + own_bias
    active = jnp.maximum(before, 0.0).astype(bf16)
    out_part = mm(active, w_reduce, NT).astype(bf16)
    grad_before = jnp.where(before > 0.0, mm(all_cotan, w_reduce, NN), 0.0)
    before_grad_b = grad_before.astype(bf16)
    second_part = mm(before_grad_b, w_expand, NT).astype(bf16)

    expand_term = mm(all_second, before_grad_b, TN).astype(bf16)
    reduce_term = mm(all_cotan, active, TN).astype(bf16)
    second_parts, expand_total, reduce_total = exchange(
        3,
        ("za2a", second_part.reshape(group_count, token_count, width)),
        ("dpscatter", expand_term[None]),
        ("dpscatter", reduce_term[None]),
    )
    grad_second = jnp.sum(second_parts.astype(jnp.float32), axis=0)
    grad_middle = cotangent + norm_backward(
        grad_second * vectors[5], normed_second, inverse_second
    )
    middle_b = grad_middle.astype(bf16)
    grad_attended = mm(middle_b, w_output, NT).astype(bf16)
    attended_heads = grad_attended.reshape(token_count, HEADS, head_size)
    grad_probs = jnp.einsum(
        "qhd,khd->hqk", attended_heads, value_heads, preferred_element_type=jnp.float32
    )
    grad_value = jnp.einsum(
        "hqk,qhd->khd", probs_b, attended_heads, preferred_element_type=jnp.float32
    )
    delta = jnp.sum(probs * grad_probs, axis=2, keepdims=True)
    grad_scores = (probs * (grad_probs - delta)).astype(bf16)
    grad_query = (
        jnp.einsum("hqk,khd->qhd", grad_scores, key_heads, preferred_element_type=jnp.float32)
        * scale
    )
    grad_key = jnp.einsum(
        "hqk,qhd->khd", grad_scores, query_heads, preferred_element_type=jnp.float32
    )
    query_grad = grad_query.reshape(token_count, width)
    key_grad = grad_key.reshape(token_count, width)
    value_grad = grad_value.reshape(token_count, width)
    query_grad_b = query_grad.astype(bf16)
    key_grad_b = key_grad.astype(bf16)
    value_grad_b = value_grad.astype(bf16)

    left, right = exchange(
        4,
        ("za2a", jnp.stack([hidden_first, hidden_first, hidden_first, attended])),
        ("za2a", jnp.stack([query_grad_b, key_grad_b, value_grad_b, middle_b])),
    )
    grad_first = (
        mm(query_grad_b, w_query, NT) + mm(key_grad_b, w_key, NT) + mm(value_grad_b, w_value, NT)
    )
    input_grad = grad_middle + norm_backward(grad_first * vectors[0], normed_first, inverse_first)
    small_terms = jnp.stack(
        [
            jnp.sum(grad_first * normed_first, axis=0),
            jnp.sum(grad_first, axis=0),
            jnp.sum(query_grad, axis=0),
            jnp.sum(value_grad, axis=0),
            jnp.sum(grad_middle, axis=0),
            jnp.sum(grad_second * normed_second, axis=0),
            jnp.sum(grad_second, axis=0),
            jnp.sum(cotangent, axis=0),
        ]
    )
    owner_mask = jnp.arange(group_count, dtype=jnp.int32) == own_index
    bias_terms = jnp.where(owner_mask[:, None], jnp.sum(grad_before, axis=0)[None], 0.0)
    vector_terms = jnp.concatenate([small_terms, bias_terms.reshape(-1, width)], axis=0)
    attn_term = mm(left.reshape(-1, width), right.reshape(-1, width), TN).astype(bf16)
    vector_all, attn_total, out_parts = exchange(
        5,
        ("dpag", vector_terms),
        ("dpscatter", attn_term[None]),
        ("za2a", out_part.reshape(group_count, token_count, width)),
    )
    outputs = middle + jnp.sum(out_parts.astype(jnp.float32), axis=0) + vectors[7]
    total_tokens = float(token_count * dp_count * group_count)
    attn_grads = attn_total / total_tokens
    ffn_grads = jnp.concatenate([expand_total, reduce_total], axis=0) / total_tokens
    attn_next = momentum_rate * attn_momenta + attn_grads
    ffn_next = momentum_rate * ffn_momenta + ffn_grads
    own_next = jnp.concatenate([attn_next, ffn_next], axis=0)
    squares = jnp.sum(own_next * own_next, axis=(1, 2))
    squares = jnp.broadcast_to(jnp.pad(squares, (0, 5))[:, None], (8, 128))

    next_full, square_all, vector_groups = exchange(
        6, ("dprow", own_next.astype(bf16)), ("dpag", squares), ("zag", jnp.sum(vector_all, axis=0))
    )
    square_plane = jnp.sum(square_all, axis=0)
    own_b = own_next.astype(bf16)
    gram_part = jnp.concatenate([mm(own_b[1], next_full[1], NT), mm(own_b[2], next_full[2], NT)])
    piece = 2 * own_count // group_count
    gram_pieces, square_groups = exchange(
        7,
        ("za2a", gram_part.astype(bf16).reshape(group_count, piece, width)),
        ("zag", square_plane),
    )
    ffn_square = jnp.sum(square_groups, axis=0)[1:3, 0]
    attn_scale = 1.0 / (jnp.sqrt(square_plane[0, 0]) + 1e-07)
    ffn_scale = 1.0 / (jnp.sqrt(ffn_square) + 1e-07)
    piece_scale = jnp.where(own_index < group_count // 2, ffn_scale[0], ffn_scale[1])
    gram_piece = (jnp.sum(gram_pieces.astype(jnp.float32), axis=0) * (piece_scale * piece_scale)).astype(bf16)
    (gram_full,) = exchange(8, (("chain", 2), gram_piece))

    row_start = dp_index * own_count
    attn_unit = next_full[0].astype(jnp.float32) * attn_scale
    attn_unit_b = attn_unit.astype(bf16)
    attn_gram = mm(attn_unit_b, attn_unit_b, NT)
    steps = [newton_schulz_rows(attn_gram, own_next[0] * attn_scale, attn_unit_b, row_start)]
    for i in range(2):
        unit_b = (next_full[1 + i].astype(jnp.float32) * ffn_scale[i]).astype(bf16)
        steps.append(
            newton_schulz_rows(
                gram_full[i].astype(jnp.float32), own_next[1 + i] * ffn_scale[i], unit_b, row_start
            )
        )
    new_attn_weights = attn_weights - muon_rate * steps[0][None]
    new_ffn_weights = ffn_weights - muon_rate * jnp.stack(steps[1:])
    vector_grads = jnp.sum(vector_groups, axis=0) / total_tokens
    new_vector_momenta = momentum_rate * vector_momenta + vector_grads
    mean_square = jnp.mean(new_vector_momenta * new_vector_momenta, axis=1, keepdims=True)
    new_vectors = vectors - vector_rate * new_vector_momenta * lax.rsqrt(mean_square + 1e-06)
    return (
        outputs,
        input_grad,
        attn_grads,
        ffn_grads,
        vector_grads,
        new_attn_weights,
        attn_next,
        new_ffn_weights,
        ffn_next,
        new_vectors,
        new_vector_momenta,
    )


def solution(mesh):
    in_specs = (
        P(("dp", "group"), None),
        P(("dp", "group"), None),
        P(("dp", "group"), None),
        P("group", "dp", None),
        P("group", "dp", None),
        P(None, "dp", "group"),
        P(None, "dp", "group"),
        P(),
        P(),
    )
    out_specs = (
        P(("dp", "group"), None),
        P(("dp", "group"), None),
        P("group", "dp", None),
        P(None, "dp", "group"),
        P(),
        P("group", "dp", None),
        P("group", "dp", None),
        P(None, "dp", "group"),
        P(None, "dp", "group"),
        P(),
        P(),
    )
    return jax.shard_map(
        on_device, mesh=mesh, in_specs=in_specs, out_specs=out_specs, check_vma=False
    )
```
